32 devices in a mesh: dp: 8 (over z, y), mp: 4 (over x, core).
Axes of the slice: x: 2, y: 2, z: 4, core: 2. Of those that a mesh axis runs over, the one named last changes fastest.
Arguments:
- tokens: bfloat16 [4096, 2048], P('dp'), may hold values from -6 to 6
- text: bfloat16 [2048, 4096], P('dp', 'mp'), may hold values from -6 to 6
- image_seg: int32 [8, 512], P('dp'), may hold values from 0 to 1, never falling along the last dimension, each value on 1 to 320 neighbouring positions
- text_seg: int32 [8, 256], P('dp'), may hold values from 0 to 1, never falling along the last dimension, each value on 1 to 160 neighbouring positions
- w_qkv: bfloat16 [3, 2048, 2048], P(None, 'dp', 'mp'), may hold values from -0.125 to 0.125
- w_out: bfloat16 [2048, 2048], P('mp', 'dp'), may hold values from -1 to 1
- c_q: bfloat16 [2048, 2048], P('dp', 'mp'), may hold values from -0.125 to 0.125
- c_kv: bfloat16 [2, 4096, 2048], P(None, 'dp', 'mp'), may hold values from -0.09375 to 0.09375
- c_out: bfloat16 [2048, 2048], P('mp', 'dp'), may hold values from -1 to 1
- w_up: bfloat16 [2048, 8192], P('dp', 'mp'), may hold values from -0.125 to 0.125
- w_down: bfloat16 [8192, 2048], P('mp', 'dp'), may hold values from -0.0625 to 0.0625
- norm_gain: float32 [4, 2048], replicated, may hold values from 0.25 to 1.75
- norm_bias: float32 [4, 2048], replicated, may hold values from -4 to 4
- out_bias: float32 [3, 2048], replicated, may hold values from -4 to 4
- up_bias: float32 [8192], P('mp'), may hold values from -4 to 4
- cotangent: bfloat16 [4096, 2048], P('dp'), may hold values from -6 to 6
Outputs:
- output: bfloat16 [4096, 2048], P('dp')
- grad_tokens: float32 [4096, 2048], P('dp')
- grad_text: float32 [2048, 4096], P('dp', 'mp')
- grad_w_qkv: float32 [3, 2048, 2048], P(None, 'dp', 'mp')
- grad_w_out: float32 [2048, 2048], P('mp', 'dp')
- grad_c_q: float32 [2048, 2048], P('dp', 'mp')
- grad_c_kv: float32 [2, 4096, 2048], P(None, 'dp', 'mp')
- grad_c_out: float32 [2048, 2048], P('mp', 'dp')
- grad_w_up: float32 [2048, 8192], P('dp', 'mp')
- grad_w_down: float32 [8192, 2048], P('mp', 'dp')
- grad_norm_gain: float32 [4, 2048], replicated
- grad_norm_bias: float32 [4, 2048], replicated
- grad_out_bias: float32 [3, 2048], replicated
- grad_up_bias: float32 [8192], P('mp')
The draws below stay inside these ranges and needn't reach their ends.
Inputs may be any that keep to these rules, and one draw needn't show every extreme that they name: In each row image_seg is 0 on the first image and 1 on the second; both images are present, and none has more than 320 tokens. In each row text_seg is 0 on the first caption and 1 on the second; both captions are present, and none has more than 160 tokens.
All inputs are finite; a program needn't handle non-finite values.
Results may differ from the reference program's by a relative error of at most 0.02.
Values may be sent and summed in bfloat16 or wider, within the bound.
No kernel may reach another device: no remote copies, remote signals or barrier semaphores. Data moves between devices by JAX's collectives and lax.ppermute only.
A program may use at most 256 MiB of HBM per device.

```python
import math
import jax
import jax.numpy as jnp
import numpy as np
from jax import lax

D = 2048
H = 16
HD = 128
FF = 8192
TW = 4096
SEQ = 512
TT = 256
HH = 2048
ROWS = 8
TOKENS = 4096
TEXT_TOKENS = 2048
IMG_MOST = 320
TXT_MOST = 160


def steps_of(key, shape, split, smallest, top_value):
    level, own = 1.0, jax.random.fold_in(key, 6)
    for dim, shards_of in split:
        draws = jnp.exp(jax.random.uniform(jax.random.fold_in(own, dim), (shards_of,), jnp.float32, smallest / len(split), top_value / len(split)))
        level = level * jnp.repeat(draws, shape[dim] // shards_of).reshape([-1 if axis == dim else 1 for axis in range(len(shape))])
    return level


def length_profile(count, total, most, slope):
    loads = [(1 << 20) // math.isqrt(grade ** slope) + 1 for grade in range(2, count + 1)]
    surplus, given = total - most - (count - 1), [1] * (count - 1)
    while surplus > 0:
        candidates = [i for i in range(count - 1) if given[i] < most]
        whole, budget = sum([loads[i] for i in candidates]), surplus
        for i in candidates:
            extra = min(most - given[i], max(1, budget * loads[i] // whole), surplus)
            given[i] = given[i] + extra
            surplus = surplus - extra
    return np.array([most] + given)


def uneven(stream_key, count, total, most, slope):
    if count == 2:
        one = jax.random.randint(stream_key, (), max(1, total - most), min(most, total - 1) + 1)
        return jnp.stack([one, total - one])
    lengths = jnp.asarray(length_profile(count, total, most, slope), jnp.int32)
    couples = (count - 1) // 2
    donor, taker = lengths[1:1 + 2 * couples:2], lengths[2:2 + 2 * couples:2]
    room = jnp.minimum(donor - 1, most - taker)
    moved = jax.random.randint(jax.random.fold_in(stream_key, 1), (couples,), 0, 1 << 20) % (room + 1)
    lengths = lengths.at[1:1 + 2 * couples:2].set(donor - moved).at[2:2 + 2 * couples:2].set(taker + moved)
    return lengths[jax.random.permutation(jax.random.fold_in(stream_key, 2), count)]


def normal_values(own_key, shape, width, bound, cuts=(), kind=jnp.bfloat16):
    values = width * jax.random.normal(own_key, shape, jnp.float32)
    if cuts:
        values = values * steps_of(own_key, shape, cuts, -0.22, 0.18)
    return jnp.clip(values, -bound, bound).astype(kind)


def setup_inputs(seed: int = 0) -> dict:
    streams_of = jax.random.split(jax.random.key(seed), 17)
    tokens = normal_values(streams_of[0], (TOKENS, D), 1.0, 6.0, ((0, 8),))
    text = normal_values(streams_of[1], (TEXT_TOKENS, TW), 1.0, 6.0, ((0, 8), (1, 4)))
    image_seg = jax.vmap(lambda own: jnp.searchsorted(jnp.cumsum(uneven(own, 2, SEQ, IMG_MOST, 0)), jnp.arange(SEQ), side="right"))(jax.random.split(streams_of[2], ROWS)).reshape((ROWS, SEQ)).astype(jnp.int32)
    text_seg = jax.vmap(lambda own: jnp.searchsorted(jnp.cumsum(uneven(own, 2, TT, TXT_MOST, 0)), jnp.arange(TT), side="right"))(jax.random.split(streams_of[3], ROWS)).reshape((ROWS, TT)).astype(jnp.int32)
    w_qkv = normal_values(streams_of[4], (3, D, HH), D ** -0.5, 0.125, ((1, 8), (2, 4)))
    w_out = normal_values(streams_of[5], (HH, D), (max(HH // 64, 1)) ** -0.5, 1.0, ((0, 4), (1, 8)))
    c_q = normal_values(streams_of[6], (D, HH), D ** -0.5, 0.125, ((0, 8), (1, 4)))
    c_kv = normal_values(streams_of[7], (2, TW, HH), TW ** -0.5, 0.09375, ((1, 8), (2, 4)))
    c_out = normal_values(streams_of[8], (HH, D), (max(HH // 64, 1)) ** -0.5, 1.0, ((0, 4), (1, 8)))
    w_up = normal_values(streams_of[9], (D, FF), D ** -0.5, 0.125, ((0, 8), (1, 4)))
    w_down = normal_values(streams_of[10], (FF, D), FF ** -0.5, 0.0625, ((0, 4), (1, 8)))
    norm_gain = jnp.clip(1.0 + 0.15 * jax.random.normal(streams_of[11], (4, D), jnp.float32), 0.25, 1.75)
    norm_bias = normal_values(streams_of[12], (4, D), 0.3, 4.0, (), jnp.float32)
    out_bias = normal_values(streams_of[13], (3, D), 0.3, 4.0, (), jnp.float32)
    up_bias = normal_values(streams_of[14], (FF,), 0.3, 4.0, ((0, 4),), jnp.float32)
    cotangent = normal_values(streams_of[15], (TOKENS, D), 1.0, 6.0, ((0, 8),))
    return {"tokens": tokens, "text": text, "image_seg": image_seg, "text_seg": text_seg, "w_qkv": w_qkv, "w_out": w_out, "c_q": c_q, "c_kv": c_kv, "c_out": c_out, "w_up": w_up, "w_down": w_down, "norm_gain": norm_gain, "norm_bias": norm_bias, "out_bias": out_bias, "up_bias": up_bias, "cotangent": cotangent}


@jax.custom_vjp
def low(v):
    return lax.optimization_barrier(v.astype(jnp.bfloat16)).astype(jnp.float32)

@jax.custom_vjp
def low_back(v):
    return v

def low_keep(v):
    return (low(v), None)

def low_pass(kept, grad):
    return (grad,)

def back_keep(v):
    return (v, None)

def back_low(kept, grad):
    return (low(grad),)
low.defvjp(low_keep, low_pass)
low_back.defvjp(back_keep, back_low)
eps = 1e-05
masked = -1e+30

def both_ways(values):
    return low_back(low(values))

def normalize(values, gain, shift):
    center = values - lax.optimization_barrier(jnp.mean(values, axis=-1, keepdims=True))
    spread = lax.optimization_barrier(jnp.mean(center * center, axis=-1, keepdims=True))
    return center * lax.rsqrt(spread + eps) * gain + shift

def gelu_tanh(values):
    return 0.5 * values * (1.0 + jnp.tanh(0.7978845608028654 * (values + 0.044715 * values * values * values)))

def matmul(left, right):
    return jnp.dot(left, right, precision=lax.Precision.HIGHEST)

def attend(queries, key_rows, value_rows, allowed):
    heads_q = queries.reshape(queries.shape[0], H, HD)
    heads_k = key_rows.reshape(key_rows.shape[0], H, HD)
    heads_v = value_rows.reshape(value_rows.shape[0], H, HD)
    scores = low_back(jnp.einsum('qhd,khd->hqk', heads_q, heads_k, precision=lax.Precision.HIGHEST) * HD ** (-0.5))
    scores = jnp.where(allowed[None], scores, masked)
    top = lax.optimization_barrier(jnp.max(scores, axis=-1, keepdims=True))
    expo = jnp.exp(scores - top)
    probs = low(expo / lax.optimization_barrier(jnp.sum(expo, axis=-1, keepdims=True)))
    mixed = jnp.einsum('hqk,khd->qhd', probs, heads_v, precision=lax.Precision.HIGHEST)
    return mixed.reshape(queries.shape[0], H * HD)

def layer_row(inputs, words, img_ids, cap_ids, params):
    w_qkv, w_out, c_q, c_kv, c_out, w_up, w_down, norm_gain, norm_bias, out_bias, up_bias = params
    same_image = img_ids[:, None] == img_ids[None, :]
    caption = img_ids[:, None] == cap_ids[None, :]
    hidden_one = low(normalize(inputs, norm_gain[0], norm_bias[0]))
    queries = both_ways(matmul(hidden_one, w_qkv[0]))
    key_rows = both_ways(matmul(hidden_one, w_qkv[1]))
    value_rows = both_ways(matmul(hidden_one, w_qkv[2]))
    self_mixed = both_ways(attend(queries, key_rows, value_rows, same_image))
    after_self = inputs + low_back(matmul(self_mixed, w_out)) + out_bias[0]
    hidden_two = low(normalize(after_self, norm_gain[1], norm_bias[1]))
    cross_query = both_ways(matmul(hidden_two, c_q))
    cross_keys = both_ways(matmul(words, c_kv[0]))
    cross_values = both_ways(matmul(words, c_kv[1]))
    cross_mixed = both_ways(attend(cross_query, cross_keys, cross_values, caption))
    after_cross = after_self + low_back(matmul(cross_mixed, c_out)) + out_bias[1]
    hidden_three = low(normalize(after_cross, norm_gain[2], norm_bias[2]))
    pre_act = low_back(matmul(hidden_three, w_up) + up_bias)
    activated = low(gelu_tanh(pre_act))
    after_mlp = after_cross + low_back(matmul(activated, w_down)) + out_bias[2]
    return normalize(after_mlp, norm_gain[3], norm_bias[3])

def reference(tokens, text, image_seg, text_seg, w_qkv, w_out, c_q, c_kv, c_out, w_up, w_down, norm_gain, norm_bias, out_bias, up_bias, cotangent):
    params = tuple((item.astype(jnp.float32) for item in (w_qkv, w_out, c_q, c_kv, c_out, w_up, w_down, norm_gain, norm_bias, out_bias, up_bias)))
    inputs = tokens.astype(jnp.float32).reshape(ROWS, SEQ, D)
    words = text.astype(jnp.float32).reshape(ROWS, TT, TW)

    def forward(inputs, words, params):

        def one_row(pieces):
            return layer_row(pieces[0], pieces[1], pieces[2], pieces[3], params)
        return lax.map(jax.checkpoint(one_row), (inputs, words, image_seg, text_seg))
    result, pull = jax.vjp(forward, inputs, words, params)
    grad_inputs, grad_words, grad_params = pull(cotangent.astype(jnp.float32).reshape(ROWS, SEQ, D))
    return (result.reshape(TOKENS, D).astype(jnp.bfloat16), grad_inputs.reshape(TOKENS, D), grad_words.reshape(TEXT_TOKENS, TW), grad_params[0], grad_params[1], grad_params[2], grad_params[3], grad_params[4], grad_params[5], grad_params[6], grad_params[7], grad_params[8], grad_params[9], grad_params[10])
```

```python
import jax
import jax.numpy as jnp
from jax import lax
from jax.experimental import pallas as pl
from jax.experimental.pallas import tpu as pltpu
from jax.sharding import PartitionSpec as P

HD = 128
BOTH = ("dp", "mp")

eps = 1e-05
masked = -1e30
f32 = jnp.float32
bf16 = jnp.bfloat16


def normalize(values, gain, shift):
    center = values - jnp.mean(values, axis=-1, keepdims=True)
    spread = jnp.mean(center * center, axis=-1, keepdims=True)
    return center * lax.rsqrt(spread + eps) * gain + shift


def gelu_tanh(values):
    return (
        0.5
        * values
        * (1.0 + jnp.tanh(0.7978845608028654 * (values + 0.044715 * values * values * values)))
    )


def dot(left, right, contract):
    return lax.dot_general(left, right, (contract, ((), ())), preferred_element_type=f32)


def softmax_of(q, k, q_seg, k_seg):
    scores = dot(q, k, ((1,), (1,))) * HD ** (-0.5)
    scores = jnp.where(q_seg == k_seg, scores, masked)
    top = jnp.max(scores, axis=-1, keepdims=True)
    expo = jnp.exp(scores - top)
    return expo / jnp.sum(expo, axis=-1, keepdims=True)


def forward_kernel(q_ref, k_ref, v_ref, qs_ref, ks_ref, o_ref):
    probs = softmax_of(q_ref[...], k_ref[...], qs_ref[...], ks_ref[...]).astype(bf16)
    o_ref[...] = dot(probs, v_ref[...], ((1,), (0,))).astype(bf16)


def backward_kernel(q_ref, k_ref, v_ref, g_ref, qs_ref, ks_ref, dq_ref, dk_ref, dv_ref):
    q, k, v, g = q_ref[...], k_ref[...], v_ref[...], g_ref[...]
    probs = softmax_of(q, k, qs_ref[...], ks_ref[...])
    dv_ref[...] = dot(probs.astype(bf16), g, ((0,), (0,))).astype(bf16)
    grad_probs = dot(g, v, ((1,), (1,)))
    shift = jnp.sum(probs * grad_probs, axis=-1, keepdims=True)
    grad_scores = (probs * (grad_probs - shift)).astype(bf16)
    dq_ref[...] = (dot(grad_scores, k, ((1,), (0,))) * HD ** (-0.5)).astype(bf16)
    dk_ref[...] = (dot(grad_scores, q, ((0,), (0,))) * HD ** (-0.5)).astype(bf16)


def column(rows, offset):
    return pl.BlockSpec((rows, HD), lambda h: (0, offset + h))


def whole(shape):
    return pl.BlockSpec(shape, lambda h: (0, 0))


def attend(q, q_at, k, k_at, v, v_at, q_seg, k_seg, heads):
    nq, nk = q.shape[0], k.shape[0]
    return pl.pallas_call(
        forward_kernel,
        grid=(heads,),
        in_specs=[
            column(nq, q_at),
            column(nk, k_at),
            column(nk, v_at),
            whole((nq, 1)),
            whole((1, nk)),
        ],
        out_specs=column(nq, 0),
        out_shape=jax.ShapeDtypeStruct((nq, heads * HD), bf16),
    )(q, k, v, q_seg, k_seg)


def attend_back(q, q_at, k, k_at, v, v_at, grad, q_seg, k_seg, heads):
    nq, nk = q.shape[0], k.shape[0]
    wide = heads * HD
    return pl.pallas_call(
        backward_kernel,
        grid=(heads,),
        in_specs=[
            column(nq, q_at),
            column(nk, k_at),
            column(nk, v_at),
            column(nq, 0),
            whole((nq, 1)),
            whole((1, nk)),
        ],
        out_specs=[column(nq, 0), column(nk, 0), column(nk, 0)],
        out_shape=[
            jax.ShapeDtypeStruct((nq, wide), bf16),
            jax.ShapeDtypeStruct((nk, wide), bf16),
            jax.ShapeDtypeStruct((nk, wide), bf16),
        ],
    )(q, k, v, grad, q_seg, k_seg)


def pick(values, index, axis=0):
    return lax.dynamic_index_in_dim(values, index, axis, keepdims=False)


def build(n_dp, n_mp):
    n_hi = n_dp // 4
    flip = {bit: [(i, i ^ bit) for i in range(n_dp)] for bit in (1, 2, 4)}
    core_swap = [(i, i ^ 1) for i in range(n_mp)]
    side = lambda i, m: i * n_mp + (m ^ 2)
    lower = lambda i, m: (i ^ 2) * n_mp + m
    pairs = [(i, m) for i in range(n_dp) for m in range(n_mp)]
    first_hop = [(i * n_mp + m, side(i, m) if m % 2 == 0 else lower(i, m)) for i, m in pairs]
    second_hop = [(i * n_mp + m, lower(i, m) if m % 2 == 0 else side(i, m)) for i, m in pairs]
    high_groups = [[h * 4 + low for h in range(n_hi)] for low in range(4)]

    def gather_tokens(own):
        near = lax.ppermute(own, BOTH, first_hop)
        two = jnp.concatenate([own, near], axis=0)
        four = jnp.concatenate([two, lax.ppermute(two, BOTH, second_hop)], axis=0)
        return jnp.concatenate([four, lax.ppermute(four, "mp", core_swap)], axis=0)

    def scatter_tokens(partial):
        part = partial.shape[0] // 8
        arrived = lax.ppermute(partial[4 * part :], "mp", core_swap)
        four = partial[: 4 * part].astype(f32) + arrived.astype(f32)
        arrived = lax.ppermute(four[2 * part :].astype(bf16), BOTH, second_hop)
        two = four[: 2 * part] + arrived.astype(f32)
        arrived = lax.ppermute(two[part:].astype(bf16), BOTH, first_hop)
        return two[:part] + arrived.astype(f32)

    def on_device(
        tokens,
        text,
        image_seg,
        text_seg,
        w_qkv,
        w_out,
        c_q,
        c_kv,
        c_out,
        w_up,
        w_down,
        norm_gain,
        norm_bias,
        out_bias,
        up_bias,
        cotangent,
    ):
        d, m = lax.axis_index("dp"), lax.axis_index("mp")
        high, low, near_y = d // 4, (d // 2) % 2, d % 2
        core = m % 2
        seq, dim = tokens.shape
        text_len = text_seg.shape[1]
        block = seq // 8
        place = low * 4 + m

        def ordered(mine, theirs, axis=0):
            return jnp.where(
                low == 0, jnp.stack([mine, theirs], axis), jnp.stack([theirs, mine], axis)
            )

        def swap_low(values):
            return lax.ppermute(values, "dp", flip[2])

        def spread(halves):
            rows, wide = halves.shape[1:]
            pair = ordered(pick(halves, low), swap_low(pick(halves, 1 - low)))
            if n_hi == 2:
                far = lax.ppermute(pair, "dp", flip[4])
                pair_y = lax.ppermute(pair, "dp", flip[1])
                far_y = lax.ppermute(far, "dp", flip[1])
                full = jnp.zeros((2, 2, 2, rows, wide), halves.dtype)
                for piece, h, y in (
                    (pair, high, near_y),
                    (far, 1 - high, near_y),
                    (pair_y, high, 1 - near_y),
                    (far_y, 1 - high, 1 - near_y),
                ):
                    full = lax.dynamic_update_slice(full, piece[None, :, None], (h, 0, y, 0, 0))
            else:
                mine = lax.all_gather(pair, "dp", axis=0, axis_index_groups=high_groups)
                theirs = lax.ppermute(mine, "dp", flip[1])
                full = jnp.where(
                    near_y == 0, jnp.stack([mine, theirs], 2), jnp.stack([theirs, mine], 2)
                )
            return full.reshape(n_dp * rows, wide)

        def collect(grad):
            rows, wide = grad.shape[0] // n_dp, grad.shape[1]
            grad = grad.reshape(n_hi, 2, 2, rows, wide)
            arrived = lax.ppermute(pick(grad, 1 - near_y, 2), "dp", flip[1])
            total = (pick(grad, near_y, 2).astype(f32) + arrived.astype(f32)).astype(bf16)
            if n_hi == 2:
                arrived = lax.ppermute(pick(total, 1 - high), "dp", flip[4])
                total = (pick(total, high).astype(f32) + arrived.astype(f32)).astype(bf16)
            else:
                total = lax.psum_scatter(
                    total, "dp", scatter_dimension=0, axis_index_groups=high_groups
                )
            theirs = swap_low(pick(total, 1 - low))
            return ordered(pick(total, low), theirs, 1).astype(f32)

        halve = lambda v: jnp.moveaxis(v.reshape(v.shape[0], 2, v.shape[1] // 2), 1, 0)
        qkv_halves = w_qkv.reshape(3, w_qkv.shape[1], 2, w_qkv.shape[2] // 2)
        qkv_halves = qkv_halves.transpose(2, 1, 0, 3).reshape(2, w_qkv.shape[1], -1)
        kv_halves = c_kv.reshape(2, c_kv.shape[1], 2, c_kv.shape[2] // 2)
        kv_halves = kv_halves.transpose(2, 1, 0, 3).reshape(2, c_kv.shape[1], -1)
        proj_halves = jnp.concatenate([halve(w_out.T), halve(c_q), halve(c_out.T)], axis=2)
        full_qkv = spread(qkv_halves)
        full_proj = spread(proj_halves)
        full_kv = spread(kv_halves)
        full_up = spread(halve(w_up))
        full_down = spread(halve(w_down.T))
        mine = proj_halves.shape[2] // 3
        heads = mine // HD
        full_out, full_cq, full_cout = (
            full_proj[:, :mine],
            full_proj[:, mine : 2 * mine],
            full_proj[:, 2 * mine :],
        )
        hidden = full_up.shape[1]
        bias_up = lax.dynamic_slice(up_bias, (low * hidden,), (hidden,))

        local = jnp.stack([tokens, cotangent])
        own = lax.dynamic_slice(local, (0, place * block, 0), (2, block, dim))
        away = lax.dynamic_slice(
            local, (0, ((1 - low) * 4 + m) * block, 0), (2, block, dim)
        )
        both = ordered(own, swap_low(away))
        segs = jnp.concatenate([image_seg[0], text_seg[0]])
        segs = ordered(segs, swap_low(segs))
        order = jnp.where(
            core == 0,
            jnp.array([0, 2, 4, 6, 1, 5, 3, 7], jnp.int32),
            jnp.array([0, 4, 2, 6, 1, 3, 5, 7], jnp.int32),
        )
        image_ids = jnp.take(segs[:, :seq].reshape(2, 8, block), place ^ order, axis=1)
        image_ids = image_ids.reshape(2, seq)
        text_ids = segs[:, seq:]
        words = lax.all_gather(ordered(text, swap_low(text)), "mp", axis=2, tiled=True)

        rows = (0, 1)
        residual = [both[r, 0].astype(f32) for r in rows]
        upstream = [both[r, 1].astype(f32) for r in rows]
        q_ids = [image_ids[r].reshape(seq, 1) for r in rows]
        i_ids = [image_ids[r].reshape(1, seq) for r in rows]
        t_ids = [text_ids[r].reshape(1, text_len) for r in rows]

        def norm(values, which):
            out, pull = jax.vjp(normalize, values, norm_gain[which], norm_bias[which])
            return out.astype(bf16), pull

        pulls = [[None] * 2 for _ in range(4)]
        hid_one, qkv, mixed, after_self = [], [], [], []
        for r in rows:
            normed, pulls[0][r] = norm(residual[r], 0)
            hid_one.append(gather_tokens(normed))
        for r in rows:
            qkv.append(dot(hid_one[r], full_qkv, ((1,), (0,))).astype(bf16))
            mixed.append(
                attend(qkv[r], 0, qkv[r], heads, qkv[r], 2 * heads, q_ids[r], i_ids[r], heads)
            )
            partial = dot(mixed[r], full_out, ((1,), (1,))).astype(bf16)
            after_self.append(residual[r] + scatter_tokens(partial) + out_bias[0])
        hid_two, cross_q, cross_kv, cross_mixed, after_cross = [], [], [], [], []
        for r in rows:
            cross_kv.append(dot(words[r], full_kv, ((1,), (0,))).astype(bf16))
        for r in rows:
            normed, pulls[1][r] = norm(after_self[r], 1)
            hid_two.append(gather_tokens(normed))
        for r in rows:
            cross_q.append(dot(hid_two[r], full_cq, ((1,), (0,))).astype(bf16))
            cross_mixed.append(
                attend(
                    cross_q[r], 0, cross_kv[r], 0, cross_kv[r], heads, q_ids[r], t_ids[r], heads
                )
            )
            partial = dot(cross_mixed[r], full_cout, ((1,), (1,))).astype(bf16)
            after_cross.append(after_self[r] + scatter_tokens(partial) + out_bias[1])
        hid_three, pre_act, act, after_mlp = [], [], [], []
        for r in rows:
            normed, pulls[2][r] = norm(after_cross[r], 2)
            hid_three.append(gather_tokens(normed))
        for r in rows:
            pre_act.append(dot(hid_three[r], full_up, ((1,), (0,))) + bias_up)
            act.append(gelu_tanh(pre_act[r]).astype(bf16))
            partial = dot(act[r], full_down, ((1,), (1,))).astype(bf16)
            after_mlp.append(after_cross[r] + scatter_tokens(partial) + out_bias[2])

        gains, shifts, biases = [0.0] * 4, [0.0] * 4, [0.0] * 3

        def back_norm(which, r, grad):
            out, gain, shift = pulls[which][r](grad)
            gains[which] = gains[which] + gain
            shifts[which] = shifts[which] + shift
            return out

        outs, grad_mlp, low_mlp = [], [], []
        for r in rows:
            final, pulls[3][r] = norm(after_mlp[r], 3)
            outs.append(final)
            grad_mlp.append(back_norm(3, r, upstream[r]))
            biases[2] = biases[2] + jnp.sum(grad_mlp[r], axis=0)
            low_mlp.append(gather_tokens(grad_mlp[r].astype(bf16)))
        grad_pre, grad_after_cross, low_cross = [], [], []
        for r in rows:
            grad_act = dot(low_mlp[r], full_down, ((1,), (0,)))
            grad_pre.append(jax.vjp(gelu_tanh, pre_act[r])[1](grad_act)[0].astype(bf16))
            partial = dot(grad_pre[r], full_up, ((1,), (1,))).astype(bf16)
            grad_in = scatter_tokens(partial)
            grad_after_cross.append(grad_mlp[r] + back_norm(2, r, grad_in))
            biases[1] = biases[1] + jnp.sum(grad_after_cross[r], axis=0)
            low_cross.append(gather_tokens(grad_after_cross[r].astype(bf16)))

        def weight_grad(left, right):
            return (
                dot(left[0], right[0], ((0,), (0,))) + dot(left[1], right[1], ((0,), (0,)))
            ).astype(bf16)

        sum_down = collect(weight_grad(low_mlp, act))
        sum_up = collect(weight_grad(hid_three, grad_pre))
        up_grad = jnp.sum(grad_pre[0].astype(f32), axis=0) + jnp.sum(
            grad_pre[1].astype(f32), axis=0
        )
        cq_low, ckv_low, grad_after_self, low_self = [], [], [], []
        for r in rows:
            grad_mixed = dot(low_cross[r], full_cout, ((1,), (0,))).astype(bf16)
            dq, dk, dv = attend_back(
                cross_q[r],
                0,
                cross_kv[r],
                0,
                cross_kv[r],
                heads,
                grad_mixed,
                q_ids[r],
                t_ids[r],
                heads,
            )
            cq_low.append(dq)
            ckv_low.append(jnp.concatenate([dk, dv], axis=1))
            partial = dot(dq, full_cq, ((1,), (1,))).astype(bf16)
            grad_in = scatter_tokens(partial)
            grad_after_self.append(grad_after_cross[r] + back_norm(1, r, grad_in))
            biases[0] = biases[0] + jnp.sum(grad_after_self[r], axis=0)
            low_self.append(gather_tokens(grad_after_self[r].astype(bf16)))
        sum_cross = collect(
            jnp.concatenate([weight_grad(hid_two, cq_low), weight_grad(low_cross, cross_mixed)], 1)
        )
        sum_kv = collect(weight_grad([words[0], words[1]], ckv_low))
        text_term = jnp.stack([dot(ckv_low[r], full_kv, ((1,), (1,))).astype(bf16) for r in rows])
        text_term = lax.psum_scatter(text_term, "mp", scatter_dimension=2, tiled=True)
        grad_text = pick(text_term, low).astype(f32) + swap_low(
            pick(text_term, 1 - low)
        ).astype(f32)
        qkv_low, grad_tokens = [], []
        for r in rows:
            grad_mixed = dot(low_self[r], full_out, ((1,), (0,))).astype(bf16)
            dq, dk, dv = attend_back(
                qkv[r],
                0,
                qkv[r],
                heads,
                qkv[r],
                2 * heads,
                grad_mixed,
                q_ids[r],
                i_ids[r],
                heads,
            )
            qkv_low.append(jnp.concatenate([dq, dk, dv], axis=1))
            partial = dot(qkv_low[r], full_qkv, ((1,), (1,))).astype(bf16)
            grad_in = scatter_tokens(partial)
            grad_tokens.append(grad_after_self[r] + back_norm(0, r, grad_in))
        sum_out = collect(weight_grad(low_self, mixed))
        sum_qkv = collect(weight_grad(hid_one, qkv_low))

        def whole_row(pieces):
            pieces = jnp.stack(pieces)
            pieces = ordered(pick(pieces, low), swap_low(pick(pieces, 1 - low)))
            pieces = lax.all_gather(pieces, "mp", axis=1)
            return pieces.reshape(seq, dim)

        output = whole_row(outs)
        grad_tokens = whole_row([piece.astype(bf16) for piece in grad_tokens]).astype(f32)

        small = jnp.concatenate([jnp.stack(gains), jnp.stack(shifts), jnp.stack(biases)]).reshape(-1)
        ups = lax.dynamic_update_slice(
            jnp.zeros((n_mp * 2 * hidden,), f32), up_grad, ((m * 2 + low) * hidden,)
        )
        small = lax.psum(jnp.concatenate([small, ups]), BOTH)
        gain_total = small[: 4 * dim].reshape(4, dim)
        shift_total = small[4 * dim : 8 * dim].reshape(4, dim)
        bias_total = small[8 * dim : 11 * dim].reshape(3, dim)
        up_total = lax.dynamic_slice(small, (11 * dim + m * 2 * hidden,), (2 * hidden,))

        flat = lambda v: v.reshape(v.shape[0], -1)
        apart = lambda v, n: v.reshape(v.shape[0], 2, n, -1).transpose(2, 0, 1, 3)
        cross_parts = apart(sum_cross, 2)
        qkv_parts = apart(sum_qkv, 3)
        kv_parts = apart(sum_kv, 2)
        return (
            output,
            grad_tokens,
            grad_text,
            qkv_parts.reshape(w_qkv.shape),
            flat(sum_out).T,
            flat(cross_parts[0]),
            kv_parts.reshape(c_kv.shape),
            flat(cross_parts[1]).T,
            flat(sum_up),
            flat(sum_down).T,
            gain_total,
            shift_total,
            bias_total,
            up_total,
        )

    return on_device


def solution(mesh):
    in_specs = (
        P("dp", None),
        P("dp", "mp"),
        P("dp", None),
        P("dp", None),
        P(None, "dp", "mp"),
        P("mp", "dp"),
        P("dp", "mp"),
        P(None, "dp", "mp"),
        P("mp", "dp"),
        P("dp", "mp"),
        P("mp", "dp"),
        P(),
        P(),
        P(),
        P("mp"),
        P("dp", None),
    )
    out_specs = (
        P("dp", None),
        P("dp", None),
        P("dp", "mp"),
        P(None, "dp", "mp"),
        P("mp", "dp"),
        P("dp", "mp"),
        P(None, "dp", "mp"),
        P("mp", "dp"),
        P("dp", "mp"),
        P("mp", "dp"),
        P(),
        P(),
        P(),
        P("mp"),
    )
    return jax.shard_map(
        build(mesh.shape["dp"], mesh.shape["mp"]),
        mesh=mesh,
        in_specs=in_specs,
        out_specs=out_specs,
        check_vma=False,
    )
```

```python
import functools

import jax
import jax.numpy as jnp
from jax import lax
from jax.experimental import pallas as pl
from jax.experimental.pallas import tpu as pltpu
from jax.sharding import PartitionSpec as P

HD = 128
BOTH = ("dp", "mp")

eps = 1e-05
masked = -1e30
f32 = jnp.float32
bf16 = jnp.bfloat16


def normalize(values, gain, shift):
    center = values - jnp.mean(values, axis=-1, keepdims=True)
    spread = jnp.mean(center * center, axis=-1, keepdims=True)
    return center * lax.rsqrt(spread + eps) * gain + shift


def gelu_tanh(values):
    return (
        0.5
        * values
        * (1.0 + jnp.tanh(0.7978845608028654 * (values + 0.044715 * values * values * values)))
    )


def dot(left, right, contract):
    return lax.dot_general(left, right, (contract, ((), ())), preferred_element_type=f32)


def softmax_of(q, k, q_seg, k_seg):
    scores = dot(q, k, ((1,), (1,))) * HD ** (-0.5)
    scores = jnp.where(q_seg == k_seg, scores, masked)
    top = jnp.max(scores, axis=-1, keepdims=True)
    expo = jnp.exp(scores - top)
    return expo / jnp.sum(expo, axis=-1, keepdims=True)


def head_at(ref, index):
    return ref[:, index * HD : (index + 1) * HD]


def forward_kernel(heads, at, q_ref, kv_ref, qs_ref, ks_ref, o_ref):
    for h in range(heads):
        probs = softmax_of(
            head_at(q_ref, h), head_at(kv_ref, at + h), qs_ref[...], ks_ref[...]
        ).astype(bf16)
        out = dot(probs, head_at(kv_ref, at + heads + h), ((1,), (0,)))
        o_ref[:, h * HD : (h + 1) * HD] = out.astype(bf16)


def backward_kernel(heads, at, q_ref, kv_ref, g_ref, qs_ref, ks_ref, *outs):
    dq_ref, dkv_ref = outs[0], outs[-1]
    for h in range(heads):
        q, k = head_at(q_ref, h), head_at(kv_ref, at + h)
        v, g = head_at(kv_ref, at + heads + h), head_at(g_ref, h)
        probs = softmax_of(q, k, qs_ref[...], ks_ref[...])
        dv = dot(probs.astype(bf16), g, ((0,), (0,)))
        grad_probs = dot(g, v, ((1,), (1,)))
        shift = jnp.sum(probs * grad_probs, axis=-1, keepdims=True)
        grad_scores = (probs * (grad_probs - shift)).astype(bf16)
        dq = dot(grad_scores, k, ((1,), (0,))) * HD ** (-0.5)
        dk = dot(grad_scores, q, ((0,), (0,))) * HD ** (-0.5)
        for ref, index, value in (
            (dq_ref, h, dq),
            (dkv_ref, at + h, dk),
            (dkv_ref, at + heads + h, dv),
        ):
            ref[:, index * HD : (index + 1) * HD] = value.astype(bf16)


def row_block(shape, row):
    return pl.BlockSpec(shape, lambda i: (row, 0))


def attend(q, kv, row, at, q_seg, k_seg, heads):
    nq, nk = q_seg.shape[0], k_seg.shape[1]
    return pl.pallas_call(
        functools.partial(forward_kernel, heads, at),
        grid=(1,),
        in_specs=[
            row_block((nq, q.shape[1]), 0),
            row_block((nk, kv.shape[1]), row),
            row_block((nq, 1), 0),
            row_block((1, nk), 0),
        ],
        out_specs=row_block((nq, heads * HD), 0),
        out_shape=jax.ShapeDtypeStruct((nq, heads * HD), bf16),
    )(q, kv, q_seg, k_seg)


def attend_back(q, kv, row, at, grad, q_seg, k_seg, heads):
    nq, nk = q_seg.shape[0], k_seg.shape[1]
    wide = heads * HD
    shapes = [(nq, 3 * wide)] if at else [(nq, wide), (nk, 2 * wide)]
    return pl.pallas_call(
        functools.partial(backward_kernel, heads, at),
        grid=(1,),
        in_specs=[
            row_block((nq, q.shape[1]), 0),
            row_block((nk, kv.shape[1]), row),
            row_block((nq, wide), 0),
            row_block((nq, 1), 0),
            row_block((1, nk), 0),
        ],
        out_specs=[row_block(shape, 0) for shape in shapes],
        out_shape=[jax.ShapeDtypeStruct(shape, bf16) for shape in shapes],
    )(q, kv, grad, q_seg, k_seg)


def assemble_kernel(kinds, order, *refs):
    step = pl.program_id(0)
    pieces, outs = refs[:4], refs[4:]
    for index, piece in enumerate(pieces):

        @pl.when(step // 2 == index)
        def _(piece=piece):
            for unit, (which, _, column) in enumerate(kinds):
                value = piece[0, unit] if len(kinds) > 1 else piece[0]
                cols = value.shape[1]
                outs[which][:, column * cols : (column + 1) * cols] = value


def assembled(order, pieces, kinds, shapes, n_blocks):
    lead = pieces[0].shape[1:]
    zeros = (0,) * len(lead)
    in_specs = [
        pl.BlockSpec(
            (1,) + lead, lambda i, o, first=2 * index: (jnp.clip(i - first, 0, 1),) + zeros
        )
        for index in range(4)
    ]
    out_specs = []
    for index, (rows, cols) in enumerate(shapes):
        kind = [kind for which, kind, _ in kinds if which == index][0]
        if kind == "row":
            out_specs.append(pl.BlockSpec((rows // n_blocks, cols), lambda i, o: (o[i], 0)))
        else:
            out_specs.append(pl.BlockSpec((rows, cols // n_blocks), lambda i, o: (0, o[i])))
    return pl.pallas_call(
        functools.partial(assemble_kernel, kinds),
        grid_spec=pltpu.PrefetchScalarGridSpec(
            num_scalar_prefetch=1, grid=(8,), in_specs=in_specs, out_specs=out_specs
        ),
        out_shape=[jax.ShapeDtypeStruct(shape, bf16) for shape in shapes],
    )(order, *pieces)


def grad_kernel(kinds, extra, splits, order, *refs):
    step = pl.program_id(0)
    refs = list(refs)
    pairs = []
    for kind, count in kinds:
        lefts = [refs.pop(0) for _ in range(count)]
        pairs.append((kind, lefts, [refs.pop(0) for _ in range(count)]))
    added = refs.pop(0) if extra else None
    outs = [refs.pop(0) for _ in splits]
    pieces = []
    for kind, lefts, rights in pairs:
        total = 0.0
        for left, right in zip(lefts, rights):
            if kind == "row":
                total = total + dot(left[...], right[...], ((0,), (0,)))
            else:
                turned = refs.pop(0)

                @pl.when(step == 0)
                def _(turned=turned, left=left):
                    turned[...] = left[...].T

                total = total + dot(turned[...], right[...], ((1,), (0,)))
        pieces.append(total)
    value = pieces[0] if len(pieces) == 1 else jnp.concatenate(pieces, axis=1)
    if extra:
        value = value + added[0].astype(f32)
    value = value.astype(bf16)
    start = 0
    for out, size in zip(outs, splits):

        @pl.when((step >= start) & (step < start + size))
        def _(out=out):
            out[0] = value

        start += size


def grad_blocks(order, terms, n_blocks, splits, added=None):
    operands, specs, kinds, scratch, wide, high = [], [], [], [], 0, 0

    def fixed(rows, cols, row):
        return pl.BlockSpec((rows, cols), lambda i, o: (row, 0))

    def moving(rows, cols, row):
        return pl.BlockSpec((rows, cols), lambda i, o: (row, o[i]))

    for kind, lefts, rights in terms:
        kinds.append((kind, len(lefts)))
        for array, rows, row in lefts:
            cols = array.shape[1] // (n_blocks if kind == "row" else 1)
            specs.append((moving if kind == "row" else fixed)(rows, cols, row))
            operands.append(array)
            if kind == "col":
                scratch.append(pltpu.VMEM((cols, rows), bf16))
            high = cols
        for index, (array, rows, row) in enumerate(rights):
            cols = array.shape[1] // (n_blocks if kind == "col" else 1)
            specs.append((moving if kind == "col" else fixed)(rows, cols, row))
            operands.append(array)
            if index == 0:
                wide += cols
    if added is not None:
        operands.append(added)
        specs.append(pl.BlockSpec((1, high, wide), lambda i, o: (i, 0, 0)))
    outs, start = [], 0
    for size in splits:
        place = lambda i, o, a=start, n=size: (jnp.clip(i - a, 0, n - 1), 0, 0)
        outs.append(pl.BlockSpec((1, high, wide), place))
        start += size
    return pl.pallas_call(
        functools.partial(grad_kernel, kinds, added is not None, splits),
        grid_spec=pltpu.PrefetchScalarGridSpec(
            num_scalar_prefetch=1,
            grid=(sum(splits),),
            in_specs=specs,
            out_specs=outs,
            scratch_shapes=scratch,
        ),
        out_shape=[jax.ShapeDtypeStruct((size, high, wide), bf16) for size in splits],
    )(order, *operands)


def pick(values, index, axis=0):
    return lax.dynamic_index_in_dim(values, index, axis, keepdims=False)


def after(value, *others):
    return lax.optimization_barrier((value,) + others)[0]


def build(n_dp, n_mp):
    n_hi = n_dp // 4
    flip = {bit: [(i, i ^ bit) for i in range(n_dp)] for bit in (1, 2, 4)}
    core_swap = [(i, i ^ 1) for i in range(n_mp)]
    side_swap = [(i, i ^ 2) for i in range(n_mp)]
    side = lambda i, m: i * n_mp + (m ^ 2)
    lower = lambda i, m: (i ^ 2) * n_mp + m
    pairs = [(i, m) for i in range(n_dp) for m in range(n_mp)]
    first_hop = [(i * n_mp + m, side(i, m) if m % 2 == 0 else lower(i, m)) for i, m in pairs]
    second_hop = [(i * n_mp + m, lower(i, m) if m % 2 == 0 else side(i, m)) for i, m in pairs]
    high_groups = [[h * 4 + low for h in range(n_hi)] for low in range(4)]

    def gather_tokens(own):
        near = lax.ppermute(own, BOTH, first_hop)
        two = jnp.concatenate([own, near], axis=0)
        four = jnp.concatenate([two, lax.ppermute(two, BOTH, second_hop)], axis=0)
        return jnp.concatenate([four, lax.ppermute(four, "mp", core_swap)], axis=0)

    def scatter_tokens(left, right, contract):
        half = left.shape[0] // 2
        part = half // 4
        arrived = lax.ppermute(
            dot(left[half:], right, contract).astype(bf16), "mp", core_swap
        )
        four = dot(left[:half], right, contract) + arrived.astype(f32)
        arrived = lax.ppermute(four[2 * part :].astype(bf16), BOTH, second_hop)
        two = four[: 2 * part] + arrived.astype(f32)
        arrived = lax.ppermute(two[part:].astype(bf16), BOTH, first_hop)
        return two[:part] + arrived.astype(f32)

    def on_device(
        tokens,
        text,
        image_seg,
        text_seg,
        w_qkv,
        w_out,
        c_q,
        c_kv,
        c_out,
        w_up,
        w_down,
        norm_gain,
        norm_bias,
        out_bias,
        up_bias,
        cotangent,
    ):
        d, m = lax.axis_index("dp"), lax.axis_index("mp")
        high, low, near_y = d // 4, (d // 2) % 2, d % 2
        core = m % 2
        seq, dim = tokens.shape
        text_len, text_dim = text_seg.shape[1], text.shape[1] * n_mp
        block = seq // 8
        place = low * 4 + m
        slice_dim = dim // n_dp
        slice_text = text_dim // n_dp
        mine = w_qkv.shape[2] // 2
        hidden = w_up.shape[1] // 2
        heads = mine // HD

        def xor_order(masks):
            return (d ^ jnp.array(masks, jnp.int32)).astype(jnp.int32)

        def ordered(own, theirs, axis=0):
            return jnp.where(
                low == 0, jnp.stack([own, theirs], axis), jnp.stack([theirs, own], axis)
            )

        def swap_low(values):
            return lax.ppermute(values, "dp", flip[2])

        def cut(parts, shape):
            def side_of(g):
                pieces = []
                for weight, kind in parts:
                    axis = 0 if kind == "col" else weight.ndim - 1
                    width = weight.shape[axis] // 2
                    pieces.append(lax.dynamic_slice_in_dim(weight, g * width, width, axis))
                return (jnp.stack(pieces) if len(pieces) > 1 else pieces[0]).reshape(shape)

            return side_of(low), side_of(1 - low)

        def spread(keep, recv):
            pair = jnp.stack([keep, recv])
            if n_hi == 2:
                far = lax.all_gather(pair, "dp", axis=0, axis_index_groups=high_groups)
                far = pick(far, 1 - high)
                return [
                    pair,
                    far,
                    lax.ppermute(pair, "dp", flip[1]),
                    lax.ppermute(far, "dp", flip[1]),
                ]
            pair = jnp.where(low == 0, pair, pair[::-1])
            own = lax.all_gather(pair, "dp", axis=0, axis_index_groups=high_groups)
            theirs = lax.ppermute(own, "dp", flip[1])
            full = jnp.where(
                near_y == 0, jnp.stack([own, theirs], 2), jnp.stack([theirs, own], 2)
            )
            return full.reshape((n_dp,) + keep.shape)

        def assemble(pieces, kinds, shapes):
            units = len(kinds)
            if n_hi != 2:
                outs = [[] for _ in shapes]
                for unit, (which, kind, _) in enumerate(kinds):
                    value = pieces[:, unit] if units > 1 else pieces
                    if kind == "col":
                        value = jnp.moveaxis(value, 0, 1)
                    outs[which].append(value.reshape(shapes[which][0], -1))
                return [jnp.concatenate(out, axis=1) for out in outs]

            return assembled(xor_order([0, 2, 4, 6, 1, 3, 5, 7]), pieces, kinds, shapes, n_dp)

        def first_blocks(terms):
            if n_hi != 2:
                return ()
            return (grad_blocks(xor_order([5, 7, 1, 3]), terms, n_dp, [4])[0],)

        def second_blocks(terms, away, *gates):
            if n_hi != 2:
                return ()
            arrived = after(lax.ppermute(away[0], "dp", flip[1]), *gates)
            return tuple(grad_blocks(xor_order([4, 6, 0, 2]), terms, n_dp, [2, 2], arrived))

        def across_high(second, *gates):
            if n_hi != 2:
                return ()
            return (after(lax.ppermute(second[0], "dp", flip[4]), *gates),)

        def collected(terms, second, arrived, axis):
            if n_hi == 2:
                total = second[1].astype(f32) + arrived[0].astype(f32)
                own, theirs = total[0], swap_low(total[1].astype(bf16))
            else:
                grads = []
                for kind, lefts, rights in terms:
                    cut_of = lambda v: v[0][v[1] * v[2] : v[1] * (v[2] + 1)]
                    grad = sum(
                        dot(cut_of(left), cut_of(right), ((0,), (0,)))
                        for left, right in zip(lefts, rights)
                    ).astype(bf16)
                    if kind == "row":
                        grads.append(grad.reshape(n_dp, -1, grad.shape[1]))
                    else:
                        grads.append(
                            jnp.moveaxis(grad.reshape(grad.shape[0], n_dp, -1), 1, 0)
                        )
                grad = jnp.concatenate(grads, axis=2)
                grad = grad.reshape((n_hi, 2, 2) + grad.shape[1:])
                arrived = lax.ppermute(pick(grad, 1 - near_y, 2), "dp", flip[1])
                total = (pick(grad, near_y, 2).astype(f32) + arrived.astype(f32)).astype(bf16)
                total = lax.psum_scatter(
                    total, "dp", scatter_dimension=0, axis_index_groups=high_groups
                )
                theirs = swap_low(pick(total, 1 - low))
                own = pick(total, low).astype(f32)
            return ordered(own, theirs.astype(f32), axis)

        qkv_shape = (3, slice_dim, mine)
        stay_qkv, go_qkv = cut([(w_qkv, "row")], qkv_shape)
        got_qkv = swap_low(go_qkv)
        packed = slice_dim == mine
        if packed:
            stay_proj, go_proj = cut(
                [(w_out, "col"), (c_q, "row"), (c_out, "col")], (3, slice_dim, mine)
            )
        else:
            singles = [
                cut([(w_out, "col")], (mine, slice_dim)),
                cut([(c_q, "row")], (slice_dim, mine)),
                cut([(c_out, "col")], (mine, slice_dim)),
            ]
        stay_kv, go_kv = cut([(c_kv, "row")], (2, slice_text, mine))
        stay_up, go_up = cut([(w_up, "row")], (slice_dim, hidden))
        stay_down, go_down = cut([(w_down, "col")], (hidden, slice_dim))
        pieces_qkv = spread(stay_qkv, got_qkv)
        far = lambda pieces, *which: tuple(pieces[i] for i in which) if n_hi == 2 else ()
        full_qkv = assemble(pieces_qkv, [(0, "row", j) for j in range(3)], [(dim, 3 * mine)])[0]
        kinds, shapes = ("col", "row", "col"), [(mine, dim), (dim, mine), (mine, dim)]
        if packed:
            got_proj = swap_low(after(go_proj, got_qkv))
            pieces_proj = spread(stay_proj, got_proj)
            full_out, full_cq, full_cout = assemble(
                pieces_proj, [(i, kind, 0) for i, kind in enumerate(kinds)], shapes
            )
        else:
            got_proj = got_qkv
            pieces_proj = [got_qkv] * 2
            full_out, full_cq, full_cout = [
                assemble(spread(stay, swap_low(go)), [(0, kind, 0)], [shape])[0]
                for (stay, go), kind, shape in zip(singles, kinds, shapes)
            ]
        got_kv = swap_low(after(go_kv, got_proj))
        pieces_kv = spread(stay_kv, got_kv)
        full_kv = assemble(pieces_kv, [(0, "row", 0), (0, "row", 1)], [(text_dim, 2 * mine)])[0]
        bias_up = lax.dynamic_slice(up_bias, (low * hidden,), (hidden,))

        local = after(jnp.stack([tokens, cotangent]), got_qkv)
        own = lax.dynamic_slice(local, (0, place * block, 0), (2, block, dim))
        away = lax.dynamic_slice(
            local, (0, ((1 - low) * 4 + m) * block, 0), (2, block, dim)
        )
        both = ordered(own, swap_low(away))
        segs = jnp.concatenate([image_seg[0], text_seg[0]])
        segs = ordered(segs, swap_low(segs))
        order = jnp.where(
            core == 0,
            jnp.array([0, 2, 4, 6, 1, 5, 3, 7], jnp.int32),
            jnp.array([0, 4, 2, 6, 1, 3, 5, 7], jnp.int32),
        )
        image_ids = jnp.take(segs[:, :seq].reshape(2, 8, block), place ^ order, axis=1)
        image_ids = image_ids.reshape(2, seq)
        text_ids = segs[:, seq:]
        words = lax.all_gather(ordered(text, swap_low(text)), "mp", axis=2, tiled=True)
        words = words.reshape(2 * text_len, text_dim)

        rows = (0, 1)
        residual = [both[r, 0].astype(f32) for r in rows]
        upstream = [both[r, 1].astype(f32) for r in rows]
        q_ids = [image_ids[r].reshape(seq, 1) for r in rows]
        i_ids = [image_ids[r].reshape(1, seq) for r in rows]
        t_ids = [text_ids[r].reshape(1, text_len) for r in rows]

        def norm(values, which):
            out, pull = jax.vjp(normalize, values, norm_gain[which], norm_bias[which])
            return out.astype(bf16), pull

        straight, across = ((1,), (0,)), ((1,), (1,))
        pulls = [[None] * 2 for _ in range(4)]
        hid_one, qkv, mixed, after_self = [], [], [], []
        for r in rows:
            normed, pulls[0][r] = norm(residual[r], 0)
            hid_one.append(gather_tokens(normed))
        hid_one[0] = after(hid_one[0], got_kv)
        got_up = swap_low(after(go_up, hid_one[1]))
        got_down = swap_low(after(go_down, hid_one[1]))
        pieces_up = spread(stay_up, got_up)
        full_up = assemble(pieces_up, [(0, "row", 0)], [(dim, hidden)])[0]
        pieces_down = spread(stay_down, got_down)
        full_down = assemble(pieces_down, [(0, "col", 0)], [(hidden, dim)])[0]
        for r in rows:
            qkv.append(dot(hid_one[r], full_qkv, straight).astype(bf16))
            mixed.append(attend(qkv[r], qkv[r], 0, heads, q_ids[r], i_ids[r], heads))
            ready = after(mixed[r], got_up, got_down, *far(pieces_kv, 1)) if r == 0 else mixed[r]
            after_self.append(
                residual[r] + scatter_tokens(ready, full_out, straight) + out_bias[0]
            )
        hid_two, cross_q, cross_mixed, after_cross = [], [], [], []
        cross_kv = dot(after(words, *far(pieces_up, 1, 2)), full_kv, straight).astype(bf16)
        for r in rows:
            normed, pulls[1][r] = norm(after_self[r], 1)
            hid_two.append(gather_tokens(after(normed, words) if r else normed))
        for r in rows:
            cross_q.append(dot(hid_two[r], full_cq, straight).astype(bf16))
            cross_mixed.append(attend(cross_q[r], cross_kv, r, 0, q_ids[r], t_ids[r], heads))
            after_cross.append(
                after_self[r] + scatter_tokens(cross_mixed[r], full_cout, straight) + out_bias[1]
            )
        hid_three, pre_act, act, after_mlp = [], [], [], []
        for r in rows:
            normed, pulls[2][r] = norm(after_cross[r], 2)
            gates = far(pieces_down, 2) if r else far(pieces_up, 3) + far(pieces_down, 1)
            hid_three.append(gather_tokens(after(normed, *gates)))
        for r in rows:
            pre_act.append(dot(hid_three[r], full_up, straight) + bias_up)
            act.append(gelu_tanh(pre_act[r]).astype(bf16))
            after_mlp.append(
                after_cross[r] + scatter_tokens(act[r], full_down, straight) + out_bias[2]
            )

        gains, shifts, biases = [0.0] * 4, [0.0] * 4, [0.0] * 3

        def back_norm(which, r, grad):
            out, gain, shift = pulls[which][r](grad)
            gains[which] = gains[which] + gain
            shifts[which] = shifts[which] + shift
            return out

        outs, grad_mlp, low_mlp = [], [], []
        for r in rows:
            final, pulls[3][r] = norm(after_mlp[r], 3)
            outs.append(final)
            grad_mlp.append(back_norm(3, r, upstream[r]))
            biases[2] = biases[2] + jnp.sum(grad_mlp[r], axis=0)
            low_mlp.append(gather_tokens(grad_mlp[r].astype(bf16)))
        def streams(values):
            return [(value, value.shape[0], 0) for value in values]

        down_term = [("col", streams(act), streams(low_mlp))]
        down = first_blocks(down_term)
        grad_pre, grad_in = [], []
        for r in rows:
            ready = low_mlp[r] if r == 0 else after(low_mlp[r], *down)
            grad_act = dot(ready, full_down, across)
            grad_pre.append(jax.vjp(gelu_tanh, pre_act[r])[1](grad_act)[0].astype(bf16))
            grad_in.append(scatter_tokens(grad_pre[r], full_up, across))
        up_term = [("row", streams(hid_three), streams(grad_pre))]
        up = first_blocks(up_term)
        grad_after_cross, low_cross = [], []
        for r in rows:
            grad_after_cross.append(grad_mlp[r] + back_norm(2, r, grad_in[r]))
            biases[1] = biases[1] + jnp.sum(grad_after_cross[r], axis=0)
            ready = grad_after_cross[r].astype(bf16)
            low_cross.append(gather_tokens(ready if r == 0 else after(ready, *up)))
        up_grad = jnp.sum(grad_pre[0].astype(f32), axis=0) + jnp.sum(
            grad_pre[1].astype(f32), axis=0
        )

        down_second = second_blocks(down_term, down, *grad_in)
        cq_low, ckv_low, grad_in = [], [], []
        for r in rows:
            ready = after(low_cross[r], *down_second) if r == 0 else low_cross[r]
            grad_mixed = dot(ready, full_cout, across).astype(bf16)
            dq, dkv = attend_back(
                cross_q[r], cross_kv, r, 0, grad_mixed, q_ids[r], t_ids[r], heads
            )
            cq_low.append(dq)
            ckv_low.append(dkv)
            grad_in.append(scatter_tokens(dq, full_cq, across))
        cq_term = ("row", streams(hid_two), streams(cq_low))
        cout_term = ("col", streams(cross_mixed), streams(low_cross))
        kv_term = [("row", [(words, text_len, r) for r in rows], streams(ckv_low))]
        both_term = [cq_term, cout_term]
        both_first, kv_first = first_blocks(both_term), first_blocks(kv_term)
        grad_after_self, low_self = [], []
        for r in rows:
            grad_after_self.append(grad_after_cross[r] + back_norm(1, r, grad_in[r]))
            biases[0] = biases[0] + jnp.sum(grad_after_self[r], axis=0)
            ready = grad_after_self[r].astype(bf16)
            if r == 1:
                up_second = second_blocks(up_term, up, *cq_low)
            gates = kv_first + up_second if r else both_first
            low_self.append(gather_tokens(after(ready, *gates)))
        text_term = dot(jnp.concatenate(ckv_low), full_kv, across).astype(bf16)

        down_far = across_high(down_second, *cq_low)
        out_term = [("col", streams(mixed), streams(low_self))]
        out_first = first_blocks(out_term)
        both_second = second_blocks(both_term, both_first, *grad_after_self)
        qkv_low = []
        for r in rows:
            gates = (*down_far, text_term, *out_first) if r else both_second
            grad_mixed = dot(after(low_self[r], *gates), full_out, across).astype(bf16)
            qkv_low.append(
                attend_back(qkv[r], qkv[r], 0, heads, grad_mixed, q_ids[r], i_ids[r], heads)[0]
            )
        qkv_term = [("row", streams(hid_one), streams(qkv_low))]
        qkv_first = first_blocks(qkv_term)
        up_far = across_high(up_second, *qkv_first)
        kv_second = second_blocks(kv_term, kv_first, *qkv_first)
        out_second = second_blocks(out_term, out_first, *kv_second)
        qkv_second = second_blocks(qkv_term, qkv_first, *out_second)
        both_far = across_high(both_second, *kv_second)
        kv_far = across_high(kv_second, *qkv_second)
        out_far = across_high(out_second, *qkv_second)
        grad_tokens = []
        for r in rows:
            grad_in = scatter_tokens(after(qkv_low[r], *qkv_first), full_qkv, across)
            piece = grad_after_self[r] + back_norm(0, r, grad_in)
            grad_tokens.append(piece)
        text_term = lax.psum_scatter(
            text_term.reshape(2, text_len, text_dim), "mp", scatter_dimension=2, tiled=True
        )
        grad_text = pick(text_term, low).astype(f32) + swap_low(
            pick(text_term, 1 - low)
        ).astype(f32)

        sum_down = collected(down_term, down_second, down_far, 0)
        sum_up = collected(up_term, up_second, up_far, 1)
        if packed:
            sum_both = collected(both_term, both_second, both_far, 0)
            sum_cq = jnp.moveaxis(sum_both[:, :, :mine], 0, 1)
            sum_cout = sum_both[:, :, mine:]
        else:
            sum_cq, sum_cout = collected([cq_term], (), (), 1), collected([cout_term], (), (), 0)
        sum_kv = collected(kv_term, kv_second, kv_far, 1)
        sum_out = collected(out_term, out_second, out_far, 0)
        sum_qkv = collected(qkv_term, qkv_second, across_high(qkv_second), 1)

        small = jnp.stack(gains + shifts + biases)
        small = small + lax.ppermute(small, "mp", core_swap)
        small = small + lax.ppermute(small, "mp", side_swap)
        wide = jnp.concatenate([small.reshape(-1), up_grad])
        if n_hi == 2:
            for bit in (1, 4):
                wide = wide + lax.ppermute(wide, "dp", flip[bit])
        else:
            wide = wide + lax.ppermute(wide, "dp", flip[1])
            wide = lax.psum(wide, "dp", axis_index_groups=high_groups)
        theirs = swap_low(wide)
        parts = (wide + theirs)[: 11 * dim].reshape(11, dim)
        up_total = ordered(wide[11 * dim :], theirs[11 * dim :]).reshape(-1)

        def whole_row(pieces):
            pieces = jnp.stack(pieces)
            pieces = ordered(pick(pieces, low), swap_low(pick(pieces, 1 - low)))
            pieces = lax.all_gather(pieces, "mp", axis=1)
            return pieces.reshape(seq, dim)

        output = whole_row(outs)
        grad_tokens = [piece.astype(bf16) for piece in grad_tokens]
        grad_tokens = whole_row([after(piece, *qkv_second) for piece in grad_tokens]).astype(f32)
        gain_total, shift_total, bias_total = parts[:4], parts[4:8], parts[8:]

        apart = lambda v, n: v.reshape(v.shape[0], 2, n, -1).transpose(2, 0, 1, 3)
        return (
            output,
            grad_tokens,
            grad_text,
            apart(sum_qkv, 3).reshape(w_qkv.shape),
            sum_out.reshape(w_out.shape),
            sum_cq.reshape(c_q.shape),
            apart(sum_kv, 2).reshape(c_kv.shape),
            sum_cout.reshape(c_out.shape),
            sum_up.reshape(w_up.shape),
            sum_down.reshape(w_down.shape),
            gain_total,
            shift_total,
            bias_total,
            up_total,
        )

    return on_device


def solution(mesh):
    in_specs = (
        P("dp", None),
        P("dp", "mp"),
        P("dp", None),
        P("dp", None),
        P(None, "dp", "mp"),
        P("mp", "dp"),
        P("dp", "mp"),
        P(None, "dp", "mp"),
        P("mp", "dp"),
        P("dp", "mp"),
        P("mp", "dp"),
        P(),
        P(),
        P(),
        P("mp"),
        P("dp", None),
    )
    out_specs = (
        P("dp", None),
        P("dp", None),
        P("dp", "mp"),
        P(None, "dp", "mp"),
        P("mp", "dp"),
        P("dp", "mp"),
        P(None, "dp", "mp"),
        P("mp", "dp"),
        P("dp", "mp"),
        P("mp", "dp"),
        P(),
        P(),
        P(),
        P("mp"),
    )
    return jax.shard_map(
        build(mesh.shape["dp"], mesh.shape["mp"]),
        mesh=mesh,
        in_specs=in_specs,
        out_specs=out_specs,
        check_vma=False,
    )
```

```python
import functools

import jax
import jax.numpy as jnp
from jax import lax
from jax.experimental.layout import Layout, with_layout_constraint
from jax.experimental import pallas as pl
from jax.experimental.pallas import tpu as pltpu
from jax.sharding import PartitionSpec as P

HD = 128
BOTH = ("dp", "mp")

eps = 1e-05
masked = -1e30
f32 = jnp.float32
bf16 = jnp.bfloat16


def normalize(values, gain, shift):
    center = values - jnp.mean(values, axis=-1, keepdims=True)
    spread = jnp.mean(center * center, axis=-1, keepdims=True)
    return center * lax.rsqrt(spread + eps) * gain + shift


def gelu_tanh(values):
    return (
        0.5
        * values
        * (1.0 + jnp.tanh(0.7978845608028654 * (values + 0.044715 * values * values * values)))
    )


def dot(left, right, contract):
    return lax.dot_general(left, right, (contract, ((), ())), preferred_element_type=f32)


def softmax_of(q, k, q_seg, k_seg):
    scores = dot(q, k, ((1,), (1,))) * HD ** (-0.5)
    scores = jnp.where(q_seg == k_seg, scores, masked)
    top = jnp.max(scores, axis=-1, keepdims=True)
    expo = jnp.exp(scores - top)
    return expo / jnp.sum(expo, axis=-1, keepdims=True)


def head_at(ref, index):
    return ref[:, index * HD : (index + 1) * HD]


def forward_kernel(heads, at, q_ref, kv_ref, qs_ref, ks_ref, o_ref):
    for h in range(heads):
        probs = softmax_of(
            head_at(q_ref, h), head_at(kv_ref, at + h), qs_ref[...], ks_ref[...]
        ).astype(bf16)
        out = dot(probs, head_at(kv_ref, at + heads + h), ((1,), (0,)))
        o_ref[:, h * HD : (h + 1) * HD] = out.astype(bf16)


def backward_kernel(heads, at, q_ref, kv_ref, g_ref, qs_ref, ks_ref, *outs):
    dq_ref, dkv_ref = outs[0], outs[-1]
    for h in range(heads):
        q, k = head_at(q_ref, h), head_at(kv_ref, at + h)
        v, g = head_at(kv_ref, at + heads + h), head_at(g_ref, h)
        probs = softmax_of(q, k, qs_ref[...], ks_ref[...])
        dv = dot(probs.astype(bf16), g, ((0,), (0,)))
        grad_probs = dot(g, v, ((1,), (1,)))
        shift = jnp.sum(probs * grad_probs, axis=-1, keepdims=True)
        grad_scores = (probs * (grad_probs - shift)).astype(bf16)
        dq = dot(grad_scores, k, ((1,), (0,))) * HD ** (-0.5)
        dk = dot(grad_scores, q, ((0,), (0,))) * HD ** (-0.5)
        for ref, index, value in (
            (dq_ref, h, dq),
            (dkv_ref, at + h, dk),
            (dkv_ref, at + heads + h, dv),
        ):
            ref[:, index * HD : (index + 1) * HD] = value.astype(bf16)


def row_block(shape, row):
    return pl.BlockSpec(shape, lambda i: (row, 0))


def attend(q, kv, row, at, q_seg, k_seg, heads):
    nq, nk = q_seg.shape[0], k_seg.shape[1]
    return pl.pallas_call(
        functools.partial(forward_kernel, heads, at),
        grid=(1,),
        in_specs=[
            row_block((nq, q.shape[1]), 0),
            row_block((nk, kv.shape[1]), row),
            row_block((nq, 1), 0),
            row_block((1, nk), 0),
        ],
        out_specs=row_block((nq, heads * HD), 0),
        out_shape=jax.ShapeDtypeStruct((nq, heads * HD), bf16),
    )(q, kv, q_seg, k_seg)


def attend_back(q, kv, row, at, grad, q_seg, k_seg, heads):
    nq, nk = q_seg.shape[0], k_seg.shape[1]
    wide = heads * HD
    shapes = [(nq, 3 * wide)] if at else [(nq, wide), (nk, 2 * wide)]
    return pl.pallas_call(
        functools.partial(backward_kernel, heads, at),
        grid=(1,),
        in_specs=[
            row_block((nq, q.shape[1]), 0),
            row_block((nk, kv.shape[1]), row),
            row_block((nq, wide), 0),
            row_block((nq, 1), 0),
            row_block((1, nk), 0),
        ],
        out_specs=[row_block(shape, 0) for shape in shapes],
        out_shape=[jax.ShapeDtypeStruct(shape, bf16) for shape in shapes],
    )(q, kv, grad, q_seg, k_seg)


def assemble_kernel(kinds, order, *refs):
    step = pl.program_id(0)
    pieces, outs = refs[:4], refs[4:]
    for index, piece in enumerate(pieces):

        @pl.when(step // 2 == index)
        def _(piece=piece):
            for unit, (which, _, column) in enumerate(kinds):
                value = piece[0, unit] if len(kinds) > 1 else piece[0]
                cols = value.shape[1]
                outs[which][:, column * cols : (column + 1) * cols] = value


def assembled(order, pieces, kinds, shapes, n_blocks):
    lead = pieces[0].shape[1:]
    zeros = (0,) * len(lead)
    in_specs = [
        pl.BlockSpec(
            (1,) + lead, lambda i, o, first=2 * index: (jnp.clip(i - first, 0, 1),) + zeros
        )
        for index in range(4)
    ]
    out_specs = []
    for index, (rows, cols) in enumerate(shapes):
        kind = [kind for which, kind, _ in kinds if which == index][0]
        if kind == "row":
            out_specs.append(pl.BlockSpec((rows // n_blocks, cols), lambda i, o: (o[i], 0)))
        else:
            out_specs.append(pl.BlockSpec((rows, cols // n_blocks), lambda i, o: (0, o[i])))
    return pl.pallas_call(
        functools.partial(assemble_kernel, kinds),
        grid_spec=pltpu.PrefetchScalarGridSpec(
            num_scalar_prefetch=1, grid=(8,), in_specs=in_specs, out_specs=out_specs
        ),
        out_shape=[jax.ShapeDtypeStruct(shape, bf16) for shape in shapes],
    )(order, *pieces)


def grad_kernel(kinds, extra, splits, order, *refs):
    step = pl.program_id(0)
    refs = list(refs)
    pairs = []
    for kind, count in kinds:
        lefts = [refs.pop(0) for _ in range(count)]
        pairs.append((kind, lefts, [refs.pop(0) for _ in range(count)]))
    added = refs.pop(0) if extra else None
    outs = [refs.pop(0) for _ in splits]
    pieces = []
    for kind, lefts, rights in pairs:
        total = 0.0
        for left, right in zip(lefts, rights):
            if kind == "row":
                total = total + dot(left[...], right[...], ((0,), (0,)))
            else:
                turned = refs.pop(0)

                @pl.when(step == 0)
                def _(turned=turned, left=left):
                    turned[...] = left[...].T

                total = total + dot(turned[...], right[...], ((1,), (0,)))
        pieces.append(total)
    value = pieces[0] if len(pieces) == 1 else jnp.concatenate(pieces, axis=1)
    if extra:
        value = value + added[0].astype(f32)
    value = value.astype(bf16)
    start = 0
    for out, size in zip(outs, splits):

        @pl.when((step >= start) & (step < start + size))
        def _(out=out):
            out[0] = value

        start += size


def grad_blocks(order, terms, n_blocks, splits, added=None):
    operands, specs, kinds, scratch, wide, high = [], [], [], [], 0, 0

    def fixed(rows, cols, row):
        return pl.BlockSpec((rows, cols), lambda i, o: (row, 0))

    def moving(rows, cols, row):
        return pl.BlockSpec((rows, cols), lambda i, o: (row, o[i]))

    for kind, lefts, rights in terms:
        kinds.append((kind, len(lefts)))
        for array, rows, row in lefts:
            cols = array.shape[1] // (n_blocks if kind == "row" else 1)
            specs.append((moving if kind == "row" else fixed)(rows, cols, row))
            operands.append(array)
            if kind == "col":
                scratch.append(pltpu.VMEM((cols, rows), bf16))
            high = cols
        for index, (array, rows, row) in enumerate(rights):
            cols = array.shape[1] // (n_blocks if kind == "col" else 1)
            specs.append((moving if kind == "col" else fixed)(rows, cols, row))
            operands.append(array)
            if index == 0:
                wide += cols
    if added is not None:
        operands.append(added)
        specs.append(pl.BlockSpec((1, high, wide), lambda i, o: (i, 0, 0)))
    outs, start = [], 0
    for size in splits:
        place = lambda i, o, a=start, n=size: (jnp.clip(i - a, 0, n - 1), 0, 0)
        outs.append(pl.BlockSpec((1, high, wide), place))
        start += size
    return pl.pallas_call(
        functools.partial(grad_kernel, kinds, added is not None, splits),
        grid_spec=pltpu.PrefetchScalarGridSpec(
            num_scalar_prefetch=1,
            grid=(sum(splits),),
            in_specs=specs,
            out_specs=outs,
            scratch_shapes=scratch,
        ),
        out_shape=[jax.ShapeDtypeStruct((size, high, wide), bf16) for size in splits],
    )(order, *operands)


def pick(values, index, axis=0):
    return lax.dynamic_index_in_dim(values, index, axis, keepdims=False)


def after(value, *others):
    return lax.optimization_barrier((value,) + others)[0]


def build(n_dp, n_mp):
    n_hi = n_dp // 4
    flip = {bit: [(i, i ^ bit) for i in range(n_dp)] for bit in (1, 2, 4)}
    core_swap = [(i, i ^ 1) for i in range(n_mp)]
    side_swap = [(i, i ^ 2) for i in range(n_mp)]
    side = lambda i, m: i * n_mp + (m ^ 2)
    lower = lambda i, m: (i ^ 2) * n_mp + m
    pairs = [(i, m) for i in range(n_dp) for m in range(n_mp)]
    first_hop = [(i * n_mp + m, side(i, m) if m % 2 == 0 else lower(i, m)) for i, m in pairs]
    second_hop = [(i * n_mp + m, lower(i, m) if m % 2 == 0 else side(i, m)) for i, m in pairs]
    high_groups = [[h * 4 + low for h in range(n_hi)] for low in range(4)]
    data_groups = [
        [h * 4 + low * 2 + y for h in range(n_hi) for y in range(2)] for low in range(2)
    ]

    def gather_tokens(own):
        near = lax.ppermute(own, BOTH, first_hop)
        two = jnp.concatenate([own, near], axis=0)
        four = jnp.concatenate([two, lax.ppermute(two, BOTH, second_hop)], axis=0)
        return jnp.concatenate([four, lax.ppermute(four, "mp", core_swap)], axis=0)

    def scatter_tokens(left, right, contract):
        half = left.shape[0] // 2
        part = half // 4
        arrived = lax.ppermute(
            dot(left[half:], right, contract).astype(bf16), "mp", core_swap
        )
        four = dot(left[:half], right, contract) + arrived.astype(f32)
        arrived = lax.ppermute(four[2 * part :].astype(bf16), BOTH, second_hop)
        two = four[: 2 * part] + arrived.astype(f32)
        arrived = lax.ppermute(two[part:].astype(bf16), BOTH, first_hop)
        return two[:part] + arrived.astype(f32)

    def on_device(
        tokens,
        text,
        image_seg,
        text_seg,
        w_qkv,
        w_out,
        c_q,
        c_kv,
        c_out,
        w_up,
        w_down,
        norm_gain,
        norm_bias,
        out_bias,
        up_bias,
        cotangent,
    ):
        d, m = lax.axis_index("dp"), lax.axis_index("mp")
        high, low, near_y = d // 4, (d // 2) % 2, d % 2
        core = m % 2
        seq, dim = tokens.shape
        text_len, text_dim = text_seg.shape[1], text.shape[1] * n_mp
        block = seq // 8
        place = low * 4 + m
        slice_dim = dim // n_dp
        slice_text = text_dim // n_dp
        mine = w_qkv.shape[2] // 2
        hidden = w_up.shape[1] // 2
        heads = mine // HD

        def xor_order(masks):
            return (d ^ jnp.array(masks, jnp.int32)).astype(jnp.int32)

        def ordered(own, theirs, axis=0):
            return jnp.where(
                low == 0, jnp.stack([own, theirs], axis), jnp.stack([theirs, own], axis)
            )

        def swap_low(values):
            return lax.ppermute(values, "dp", flip[2])

        def cut(parts, shape):
            def side_of(g):
                pieces = []
                for weight, kind in parts:
                    axis = 0 if kind == "col" else weight.ndim - 1
                    width = weight.shape[axis] // 2
                    pieces.append(lax.dynamic_slice_in_dim(weight, g * width, width, axis))
                return (jnp.stack(pieces) if len(pieces) > 1 else pieces[0]).reshape(shape)

            return side_of(low), side_of(1 - low)

        def spread(keep, recv):
            pair = jnp.stack([keep, recv])
            if n_hi == 2:
                far = lax.all_gather(pair, "dp", axis=0, axis_index_groups=high_groups)
                far = pick(far, 1 - high)
                return [
                    pair,
                    far,
                    lax.ppermute(pair, "dp", flip[1]),
                    lax.ppermute(far, "dp", flip[1]),
                ]
            pair = jnp.where(low == 0, pair, pair[::-1])
            own = lax.all_gather(pair, "dp", axis=0, axis_index_groups=high_groups)
            theirs = lax.ppermute(own, "dp", flip[1])
            full = jnp.where(
                near_y == 0, jnp.stack([own, theirs], 2), jnp.stack([theirs, own], 2)
            )
            return full.reshape((n_dp,) + keep.shape)

        def assemble(pieces, kinds, shapes):
            units = len(kinds)
            if n_hi != 2:
                outs = [[] for _ in shapes]
                for unit, (which, kind, _) in enumerate(kinds):
                    value = pieces[:, unit] if units > 1 else pieces
                    if kind == "col":
                        value = jnp.moveaxis(value, 0, 1)
                    outs[which].append(value.reshape(shapes[which][0], -1))
                return [jnp.concatenate(out, axis=1) for out in outs]

            return assembled(xor_order([0, 2, 4, 6, 1, 3, 5, 7]), pieces, kinds, shapes, n_dp)

        def all_blocks(terms):
            if n_hi != 2:
                return ()
            j = jnp.arange(8, dtype=jnp.int32)
            order = (j // 4 * 4 + (low ^ (j % 2)) * 2 + j // 2 % 2).astype(jnp.int32)
            return (grad_blocks(order, terms, n_dp, [8])[0],)

        def scattered(terms, blocks, axis, *gates):
            if n_hi != 2:
                return collected(terms, (), (), axis)
            total = lax.psum_scatter(
                blocks[0].reshape((4, 2) + blocks[0].shape[1:]),
                "dp",
                scatter_dimension=0,
                axis_index_groups=data_groups,
            )
            total = after(with_layout_constraint(total, Layout((0, 1, 2))), *gates)
            return ordered(total[0].astype(f32), swap_low(total[1]).astype(f32), axis)

        def first_blocks(terms):
            if n_hi != 2:
                return ()
            return (grad_blocks(xor_order([5, 7, 1, 3]), terms, n_dp, [4])[0],)

        def second_blocks(terms, away, *gates):
            if n_hi != 2:
                return ()
            arrived = after(lax.ppermute(away[0], "dp", flip[1]), *gates)
            return tuple(grad_blocks(xor_order([4, 6, 0, 2]), terms, n_dp, [2, 2], arrived))

        def across_high(second, *gates):
            if n_hi != 2:
                return ()
            return (after(lax.ppermute(second[0], "dp", flip[4]), *gates),)

        def collected(terms, second, arrived, axis):
            if n_hi == 2:
                total = second[1].astype(f32) + arrived[0].astype(f32)
                own, theirs = total[0], swap_low(total[1].astype(bf16))
            else:
                grads = []
                for kind, lefts, rights in terms:
                    cut_of = lambda v: v[0][v[1] * v[2] : v[1] * (v[2] + 1)]
                    grad = sum(
                        dot(cut_of(left), cut_of(right), ((0,), (0,)))
                        for left, right in zip(lefts, rights)
                    ).astype(bf16)
                    if kind == "row":
                        grads.append(grad.reshape(n_dp, -1, grad.shape[1]))
                    else:
                        grads.append(
                            jnp.moveaxis(grad.reshape(grad.shape[0], n_dp, -1), 1, 0)
                        )
                grad = jnp.concatenate(grads, axis=2)
                grad = grad.reshape((n_hi, 2, 2) + grad.shape[1:])
                arrived = lax.ppermute(pick(grad, 1 - near_y, 2), "dp", flip[1])
                total = (pick(grad, near_y, 2).astype(f32) + arrived.astype(f32)).astype(bf16)
                total = lax.psum_scatter(
                    total, "dp", scatter_dimension=0, axis_index_groups=high_groups
                )
                theirs = swap_low(pick(total, 1 - low))
                own = pick(total, low).astype(f32)
            return ordered(own, theirs.astype(f32), axis)

        qkv_shape = (3, slice_dim, mine)
        stay_qkv, go_qkv = cut([(w_qkv, "row")], qkv_shape)
        got_qkv = swap_low(go_qkv)
        packed = slice_dim == mine
        if packed:
            stay_proj, go_proj = cut(
                [(w_out, "col"), (c_q, "row"), (c_out, "col")], (3, slice_dim, mine)
            )
        else:
            singles = [
                cut([(w_out, "col")], (mine, slice_dim)),
                cut([(c_q, "row")], (slice_dim, mine)),
                cut([(c_out, "col")], (mine, slice_dim)),
            ]
        stay_kv, go_kv = cut([(c_kv, "row")], (2, slice_text, mine))
        stay_up, go_up = cut([(w_up, "row")], (slice_dim, hidden))
        stay_down, go_down = cut([(w_down, "col")], (hidden, slice_dim))
        pieces_qkv = spread(stay_qkv, got_qkv)
        far = lambda pieces, *which: tuple(pieces[i] for i in which) if n_hi == 2 else ()
        full_qkv = assemble(pieces_qkv, [(0, "row", j) for j in range(3)], [(dim, 3 * mine)])[0]
        kinds, shapes = ("col", "row", "col"), [(mine, dim), (dim, mine), (mine, dim)]
        if packed:
            got_proj = swap_low(after(go_proj, got_qkv))
            pieces_proj = spread(stay_proj, got_proj)
            full_out, full_cq, full_cout = assemble(
                pieces_proj, [(i, kind, 0) for i, kind in enumerate(kinds)], shapes
            )
        else:
            got_proj = got_qkv
            pieces_proj = [got_qkv] * 2
            full_out, full_cq, full_cout = [
                assemble(spread(stay, swap_low(go)), [(0, kind, 0)], [shape])[0]
                for (stay, go), kind, shape in zip(singles, kinds, shapes)
            ]
        got_kv = swap_low(after(go_kv, got_proj))
        pieces_kv = spread(stay_kv, got_kv)
        full_kv = assemble(pieces_kv, [(0, "row", 0), (0, "row", 1)], [(text_dim, 2 * mine)])[0]
        bias_up = lax.dynamic_slice(up_bias, (low * hidden,), (hidden,))

        local = after(jnp.stack([tokens, cotangent]), got_qkv)
        own = lax.dynamic_slice(local, (0, place * block, 0), (2, block, dim))
        away = lax.dynamic_slice(
            local, (0, ((1 - low) * 4 + m) * block, 0), (2, block, dim)
        )
        both = ordered(own, swap_low(away))
        segs = jnp.concatenate([image_seg[0], text_seg[0]])
        segs = ordered(segs, swap_low(segs))
        order = jnp.where(
            core == 0,
            jnp.array([0, 2, 4, 6, 1, 5, 3, 7], jnp.int32),
            jnp.array([0, 4, 2, 6, 1, 3, 5, 7], jnp.int32),
        )
        image_ids = jnp.take(segs[:, :seq].reshape(2, 8, block), place ^ order, axis=1)
        image_ids = image_ids.reshape(2, seq)
        text_ids = segs[:, seq:]
        words = lax.all_gather(ordered(text, swap_low(text)), "mp", axis=2, tiled=True)
        words = words.reshape(2 * text_len, text_dim)

        rows = (0, 1)
        residual = [both[r, 0].astype(f32) for r in rows]
        upstream = [both[r, 1].astype(f32) for r in rows]
        q_ids = [image_ids[r].reshape(seq, 1) for r in rows]
        i_ids = [image_ids[r].reshape(1, seq) for r in rows]
        t_ids = [text_ids[r].reshape(1, text_len) for r in rows]

        def norm(values, which):
            out, pull = jax.vjp(normalize, values, norm_gain[which], norm_bias[which])
            return out.astype(bf16), pull

        straight, across = ((1,), (0,)), ((1,), (1,))
        pulls = [[None] * 2 for _ in range(4)]
        hid_one, qkv, mixed, after_self = [], [], [], []
        for r in rows:
            normed, pulls[0][r] = norm(residual[r], 0)
            hid_one.append(gather_tokens(normed))
        hid_one[0] = after(hid_one[0], got_kv)
        got_up = swap_low(after(go_up, hid_one[1]))
        got_down = swap_low(after(go_down, hid_one[1]))
        pieces_up = spread(stay_up, got_up)
        full_up = assemble(pieces_up, [(0, "row", 0)], [(dim, hidden)])[0]
        pieces_down = spread(stay_down, got_down)
        full_down = assemble(pieces_down, [(0, "col", 0)], [(hidden, dim)])[0]
        for r in rows:
            qkv.append(dot(hid_one[r], full_qkv, straight).astype(bf16))
            mixed.append(attend(qkv[r], qkv[r], 0, heads, q_ids[r], i_ids[r], heads))
            ready = after(mixed[r], got_up, got_down, *far(pieces_kv, 1)) if r == 0 else mixed[r]
            after_self.append(
                residual[r] + scatter_tokens(ready, full_out, straight) + out_bias[0]
            )
        hid_two, cross_q, cross_mixed, after_cross = [], [], [], []
        cross_kv = dot(after(words, *far(pieces_up, 1, 2)), full_kv, straight).astype(bf16)
        for r in rows:
            normed, pulls[1][r] = norm(after_self[r], 1)
            hid_two.append(gather_tokens(after(normed, words) if r else normed))
        for r in rows:
            cross_q.append(dot(hid_two[r], full_cq, straight).astype(bf16))
            cross_mixed.append(attend(cross_q[r], cross_kv, r, 0, q_ids[r], t_ids[r], heads))
            after_cross.append(
                after_self[r] + scatter_tokens(cross_mixed[r], full_cout, straight) + out_bias[1]
            )
        hid_three, pre_act, act, after_mlp = [], [], [], []
        for r in rows:
            normed, pulls[2][r] = norm(after_cross[r], 2)
            gates = far(pieces_down, 2) if r else far(pieces_up, 3) + far(pieces_down, 1)
            hid_three.append(gather_tokens(after(normed, *gates)))
        for r in rows:
            pre_act.append(dot(hid_three[r], full_up, straight) + bias_up)
            act.append(gelu_tanh(pre_act[r]).astype(bf16))
            after_mlp.append(
                after_cross[r] + scatter_tokens(act[r], full_down, straight) + out_bias[2]
            )

        gains, shifts, biases = [0.0] * 4, [0.0] * 4, [0.0] * 3

        def back_norm(which, r, grad):
            out, gain, shift = pulls[which][r](grad)
            gains[which] = gains[which] + gain
            shifts[which] = shifts[which] + shift
            return out

        outs, grad_mlp, low_mlp = [], [], []
        for r in rows:
            final, pulls[3][r] = norm(after_mlp[r], 3)
            outs.append(final)
            grad_mlp.append(back_norm(3, r, upstream[r]))
            biases[2] = biases[2] + jnp.sum(grad_mlp[r], axis=0)
            low_mlp.append(gather_tokens(grad_mlp[r].astype(bf16)))
        def streams(values):
            return [(value, value.shape[0], 0) for value in values]

        down_term = [("col", streams(act), streams(low_mlp))]
        down = all_blocks(down_term)
        grad_pre, grad_in = [], []
        for r in rows:
            ready = low_mlp[r] if r == 0 else after(low_mlp[r], *down)
            grad_act = dot(ready, full_down, across)
            grad_pre.append(jax.vjp(gelu_tanh, pre_act[r])[1](grad_act)[0].astype(bf16))
            grad_in.append(scatter_tokens(grad_pre[r], full_up, across))
        up_term = [("row", streams(hid_three), streams(grad_pre))]
        up = all_blocks(up_term)
        grad_after_cross, low_cross = [], []
        for r in rows:
            grad_after_cross.append(grad_mlp[r] + back_norm(2, r, grad_in[r]))
            biases[1] = biases[1] + jnp.sum(grad_after_cross[r], axis=0)
            ready = grad_after_cross[r].astype(bf16)
            low_cross.append(gather_tokens(ready if r == 0 else after(ready, *up)))
        up_grad = jnp.sum(grad_pre[0].astype(f32), axis=0) + jnp.sum(
            grad_pre[1].astype(f32), axis=0
        )

        cq_low, ckv_low, grad_in = [], [], []
        for r in rows:
            grad_mixed = dot(low_cross[r], full_cout, across).astype(bf16)
            dq, dkv = attend_back(
                cross_q[r], cross_kv, r, 0, grad_mixed, q_ids[r], t_ids[r], heads
            )
            cq_low.append(dq)
            ckv_low.append(dkv)
            grad_in.append(scatter_tokens(dq, full_cq, across))
        cq_term = ("row", streams(hid_two), streams(cq_low))
        cout_term = ("col", streams(cross_mixed), streams(low_cross))
        kv_term = [("row", [(words, text_len, r) for r in rows], streams(ckv_low))]
        both_term = [cq_term, cout_term]
        both_first, kv_first = first_blocks(both_term), all_blocks(kv_term)
        grad_after_self, low_self = [], []
        for r in rows:
            grad_after_self.append(grad_after_cross[r] + back_norm(1, r, grad_in[r]))
            biases[0] = biases[0] + jnp.sum(grad_after_self[r], axis=0)
            ready = grad_after_self[r].astype(bf16)
            gates = kv_first if r else both_first
            low_self.append(gather_tokens(after(ready, *gates)))

        keys_low = jnp.concatenate(ckv_low)
        width, x_at = text_dim // n_mp, m // 2

        def text_part(owner):
            rows_of = lax.dynamic_slice_in_dim(full_kv, owner * width, width, 0)
            return dot(keys_low, rows_of, across)

        def text_sum(side):
            away = text_part(side * 2 + 1 - core).astype(bf16)
            return text_part(side * 2 + core) + lax.ppermute(away, "mp", core_swap).astype(f32)

        arrived = lax.ppermute(text_sum(1 - x_at).astype(bf16), "mp", side_swap)
        text_total = (text_sum(x_at) + arrived.astype(f32)).reshape(2, text_len, width)
        both_second = second_blocks(both_term, both_first, *grad_after_self)
        qkv_low = []
        for r in rows:
            ready = after(low_self[r], *((text_total,) if r else both_second))
            grad_mixed = dot(ready, full_out, across).astype(bf16)
            qkv_low.append(
                attend_back(qkv[r], qkv[r], 0, heads, grad_mixed, q_ids[r], i_ids[r], heads)[0]
            )
        qkv_term = [("row", streams(hid_one), streams(qkv_low))]
        qkv_first = all_blocks(qkv_term)
        last_low = [after(low_self[0], *qkv_first), low_self[1]]
        out_term = [("col", streams(mixed), streams(last_low))]
        out_first = first_blocks(out_term)
        grad_in = []
        for r in rows:
            gates = out_first if r else qkv_first
            grad_in.append(scatter_tokens(after(qkv_low[r], *gates), full_qkv, across))
        out_second = second_blocks(out_term, out_first, grad_in[0])
        sum_down = scattered(down_term, down, 0, *grad_in)
        sum_up = scattered(up_term, up, 1, *grad_in)
        sum_kv = scattered(kv_term, kv_first, 1, *grad_in)
        grad_tokens = [grad_after_self[r] + back_norm(0, r, grad_in[r]) for r in rows]
        both_far = across_high(both_second, *grad_in)
        out_far = across_high(out_second, *grad_tokens)
        text_total = after(text_total, *grad_in)
        arrived = swap_low(pick(text_total, 1 - low).astype(bf16))
        grad_text = pick(text_total, low) + arrived.astype(f32)

        if packed:
            sum_both = collected(both_term, both_second, both_far, 0)
            sum_cq = jnp.moveaxis(sum_both[:, :, :mine], 0, 1)
            sum_cout = sum_both[:, :, mine:]
        else:
            sum_cq, sum_cout = collected([cq_term], (), (), 1), collected([cout_term], (), (), 0)
        sum_out = collected(out_term, out_second, out_far, 0)
        sum_qkv = scattered(qkv_term, qkv_first, 1)

        small = jnp.stack(gains + shifts + biases)
        small = small + lax.ppermute(small, "mp", core_swap)
        small = small + lax.ppermute(small, "mp", side_swap)
        wide = jnp.concatenate([small.reshape(-1), up_grad])
        if n_hi == 2:
            for bit in (1, 4):
                wide = wide + lax.ppermute(wide, "dp", flip[bit])
        else:
            wide = wide + lax.ppermute(wide, "dp", flip[1])
            wide = lax.psum(wide, "dp", axis_index_groups=high_groups)
        theirs = swap_low(wide)
        parts = (wide + theirs)[: 11 * dim].reshape(11, dim)
        up_total = ordered(wide[11 * dim :], theirs[11 * dim :]).reshape(-1)

        def whole_row(pieces):
            pieces = jnp.stack(pieces)
            pieces = ordered(pick(pieces, low), swap_low(pick(pieces, 1 - low)))
            pieces = lax.all_gather(pieces, "mp", axis=1)
            return pieces.reshape(seq, dim)

        output = whole_row(outs)
        grad_tokens = [piece.astype(bf16) for piece in grad_tokens]
        grad_tokens = whole_row([piece for piece in grad_tokens]).astype(f32)
        gain_total, shift_total, bias_total = parts[:4], parts[4:8], parts[8:]

        apart = lambda v, n: v.reshape(v.shape[0], 2, n, -1).transpose(2, 0, 1, 3)
        return (
            output,
            grad_tokens,
            grad_text,
            apart(sum_qkv, 3).reshape(w_qkv.shape),
            sum_out.reshape(w_out.shape),
            sum_cq.reshape(c_q.shape),
            apart(sum_kv, 2).reshape(c_kv.shape),
            sum_cout.reshape(c_out.shape),
            sum_up.reshape(w_up.shape),
            sum_down.reshape(w_down.shape),
            gain_total,
            shift_total,
            bias_total,
            up_total,
        )

    return on_device


def solution(mesh):
    in_specs = (
        P("dp", None),
        P("dp", "mp"),
        P("dp", None),
        P("dp", None),
        P(None, "dp", "mp"),
        P("mp", "dp"),
        P("dp", "mp"),
        P(None, "dp", "mp"),
        P("mp", "dp"),
        P("dp", "mp"),
        P("mp", "dp"),
        P(),
        P(),
        P(),
        P("mp"),
        P("dp", None),
    )
    out_specs = (
        P("dp", None),
        P("dp", None),
        P("dp", "mp"),
        P(None, "dp", "mp"),
        P("mp", "dp"),
        P("dp", "mp"),
        P(None, "dp", "mp"),
        P("mp", "dp"),
        P("dp", "mp"),
        P("mp", "dp"),
        P(),
        P(),
        P(),
        P("mp"),
    )
    return jax.shard_map(
        build(mesh.shape["dp"], mesh.shape["mp"]),
        mesh=mesh,
        in_specs=in_specs,
        out_specs=out_specs,
        check_vma=False,
    )
```

```python
import functools

import jax
import jax.numpy as jnp
from jax import lax
from jax.experimental.layout import Layout, with_layout_constraint
from jax.experimental import pallas as pl
from jax.experimental.pallas import tpu as pltpu
from jax.sharding import PartitionSpec as P

HD = 128
BOTH = ("dp", "mp")

eps = 1e-05
masked = -1e30
f32 = jnp.float32
bf16 = jnp.bfloat16


def normalize(values, gain, shift):
    center = values - jnp.mean(values, axis=-1, keepdims=True)
    spread = jnp.mean(center * center, axis=-1, keepdims=True)
    return center * lax.rsqrt(spread + eps) * gain + shift


def gelu_tanh(values):
    return (
        0.5
        * values
        * (1.0 + jnp.tanh(0.7978845608028654 * (values + 0.044715 * values * values * values)))
    )


def dot(left, right, contract):
    return lax.dot_general(left, right, (contract, ((), ())), preferred_element_type=f32)


def softmax_of(q, k, q_seg, k_seg):
    scores = dot(q, k, ((1,), (1,))) * HD ** (-0.5)
    scores = jnp.where(q_seg == k_seg, scores, masked)
    top = jnp.max(scores, axis=-1, keepdims=True)
    expo = jnp.exp(scores - top)
    return expo / jnp.sum(expo, axis=-1, keepdims=True)


def head_at(ref, index):
    return ref[:, index * HD : (index + 1) * HD]


def forward_kernel(heads, at, q_ref, kv_ref, qs_ref, ks_ref, o_ref):
    for h in range(heads):
        probs = softmax_of(
            head_at(q_ref, h), head_at(kv_ref, at + h), qs_ref[...], ks_ref[...]
        ).astype(bf16)
        out = dot(probs, head_at(kv_ref, at + heads + h), ((1,), (0,)))
        o_ref[:, h * HD : (h + 1) * HD] = out.astype(bf16)


def backward_kernel(heads, at, q_ref, kv_ref, g_ref, qs_ref, ks_ref, *outs):
    dq_ref, dkv_ref = outs[0], outs[-1]
    for h in range(heads):
        q, k = head_at(q_ref, h), head_at(kv_ref, at + h)
        v, g = head_at(kv_ref, at + heads + h), head_at(g_ref, h)
        probs = softmax_of(q, k, qs_ref[...], ks_ref[...])
        dv = dot(probs.astype(bf16), g, ((0,), (0,)))
        grad_probs = dot(g, v, ((1,), (1,)))
        shift = jnp.sum(probs * grad_probs, axis=-1, keepdims=True)
        grad_scores = (probs * (grad_probs - shift)).astype(bf16)
        dq = dot(grad_scores, k, ((1,), (0,))) * HD ** (-0.5)
        dk = dot(grad_scores, q, ((0,), (0,))) * HD ** (-0.5)
        for ref, index, value in (
            (dq_ref, h, dq),
            (dkv_ref, at + h, dk),
            (dkv_ref, at + heads + h, dv),
        ):
            ref[:, index * HD : (index + 1) * HD] = value.astype(bf16)


def row_block(shape, row):
    return pl.BlockSpec(shape, lambda i: (row, 0))


def attend(q, kv, row, at, q_seg, k_seg, heads):
    nq, nk = q_seg.shape[0], k_seg.shape[1]
    return pl.pallas_call(
        functools.partial(forward_kernel, heads, at),
        grid=(1,),
        in_specs=[
            row_block((nq, q.shape[1]), 0),
            row_block((nk, kv.shape[1]), row),
            row_block((nq, 1), 0),
            row_block((1, nk), 0),
        ],
        out_specs=row_block((nq, heads * HD), 0),
        out_shape=jax.ShapeDtypeStruct((nq, heads * HD), bf16),
    )(q, kv, q_seg, k_seg)


def attend_back(q, kv, row, at, grad, q_seg, k_seg, heads):
    nq, nk = q_seg.shape[0], k_seg.shape[1]
    wide = heads * HD
    shapes = [(nq, 3 * wide)] if at else [(nq, wide), (nk, 2 * wide)]
    return pl.pallas_call(
        functools.partial(backward_kernel, heads, at),
        grid=(1,),
        in_specs=[
            row_block((nq, q.shape[1]), 0),
            row_block((nk, kv.shape[1]), row),
            row_block((nq, wide), 0),
            row_block((nq, 1), 0),
            row_block((1, nk), 0),
        ],
        out_specs=[row_block(shape, 0) for shape in shapes],
        out_shape=[jax.ShapeDtypeStruct(shape, bf16) for shape in shapes],
    )(q, kv, grad, q_seg, k_seg)


def assemble_kernel(kinds, order, *refs):
    step = pl.program_id(0)
    pieces, outs = refs[:4], refs[4:]
    for index, piece in enumerate(pieces):

        @pl.when(step // 2 == index)
        def _(piece=piece):
            for unit, (which, _, column) in enumerate(kinds):
                value = piece[0, unit] if len(kinds) > 1 else piece[0]
                cols = value.shape[1]
                outs[which][:, column * cols : (column + 1) * cols] = value


def assembled(order, pieces, kinds, shapes, n_blocks):
    lead = pieces[0].shape[1:]
    zeros = (0,) * len(lead)
    in_specs = [
        pl.BlockSpec(
            (1,) + lead, lambda i, o, first=2 * index: (jnp.clip(i - first, 0, 1),) + zeros
        )
        for index in range(4)
    ]
    out_specs = []
    for index, (rows, cols) in enumerate(shapes):
        kind = [kind for which, kind, _ in kinds if which == index][0]
        if kind == "row":
            out_specs.append(pl.BlockSpec((rows // n_blocks, cols), lambda i, o: (o[i], 0)))
        else:
            out_specs.append(pl.BlockSpec((rows, cols // n_blocks), lambda i, o: (0, o[i])))
    return pl.pallas_call(
        functools.partial(assemble_kernel, kinds),
        grid_spec=pltpu.PrefetchScalarGridSpec(
            num_scalar_prefetch=1, grid=(8,), in_specs=in_specs, out_specs=out_specs
        ),
        out_shape=[jax.ShapeDtypeStruct(shape, bf16) for shape in shapes],
    )(order, *pieces)


def grad_kernel(kinds, extra, splits, order, *refs):
    step = pl.program_id(0)
    refs = list(refs)
    pairs = []
    for kind, count in kinds:
        lefts = [refs.pop(0) for _ in range(count)]
        pairs.append((kind, lefts, [refs.pop(0) for _ in range(count)]))
    added = refs.pop(0) if extra else None
    outs = [refs.pop(0) for _ in splits]
    pieces = []
    for kind, lefts, rights in pairs:
        total = 0.0
        for left, right in zip(lefts, rights):
            if kind == "row":
                total = total + dot(left[...], right[...], ((0,), (0,)))
            else:
                turned = refs.pop(0)

                @pl.when(step == 0)
                def _(turned=turned, left=left):
                    turned[...] = left[...].T

                total = total + dot(turned[...], right[...], ((1,), (0,)))
        pieces.append(total)
    value = pieces[0] if len(pieces) == 1 else jnp.concatenate(pieces, axis=1)
    if extra:
        value = value + added[0].astype(f32)
    value = value.astype(bf16)
    start = 0
    for out, size in zip(outs, splits):

        @pl.when((step >= start) & (step < start + size))
        def _(out=out):
            out[0] = value

        start += size


def grad_blocks(order, terms, n_blocks, splits, added=None):
    operands, specs, kinds, scratch, wide, high = [], [], [], [], 0, 0

    def fixed(rows, cols, row):
        return pl.BlockSpec((rows, cols), lambda i, o: (row, 0))

    def moving(rows, cols, row):
        return pl.BlockSpec((rows, cols), lambda i, o: (row, o[i]))

    for kind, lefts, rights in terms:
        kinds.append((kind, len(lefts)))
        for array, rows, row in lefts:
            cols = array.shape[1] // (n_blocks if kind == "row" else 1)
            specs.append((moving if kind == "row" else fixed)(rows, cols, row))
            operands.append(array)
            if kind == "col":
                scratch.append(pltpu.VMEM((cols, rows), bf16))
            high = cols
        for index, (array, rows, row) in enumerate(rights):
            cols = array.shape[1] // (n_blocks if kind == "col" else 1)
            specs.append((moving if kind == "col" else fixed)(rows, cols, row))
            operands.append(array)
            if index == 0:
                wide += cols
    if added is not None:
        operands.append(added)
        specs.append(pl.BlockSpec((1, high, wide), lambda i, o: (i, 0, 0)))
    outs, start = [], 0
    for size in splits:
        place = lambda i, o, a=start, n=size: (jnp.clip(i - a, 0, n - 1), 0, 0)
        outs.append(pl.BlockSpec((1, high, wide), place))
        start += size
    return pl.pallas_call(
        functools.partial(grad_kernel, kinds, added is not None, splits),
        grid_spec=pltpu.PrefetchScalarGridSpec(
            num_scalar_prefetch=1,
            grid=(sum(splits),),
            in_specs=specs,
            out_specs=outs,
            scratch_shapes=scratch,
        ),
        out_shape=[jax.ShapeDtypeStruct((size, high, wide), bf16) for size in splits],
    )(order, *operands)


def pick(values, index, axis=0):
    return lax.dynamic_index_in_dim(values, index, axis, keepdims=False)


def after(value, *others):
    return lax.optimization_barrier((value,) + others)[0]


def build(n_dp, n_mp):
    n_hi = n_dp // 4
    flip = {bit: [(i, i ^ bit) for i in range(n_dp)] for bit in (1, 2, 4)}
    core_swap = [(i, i ^ 1) for i in range(n_mp)]
    side_swap = [(i, i ^ 2) for i in range(n_mp)]
    side = lambda i, m: i * n_mp + (m ^ 2)
    lower = lambda i, m: (i ^ 2) * n_mp + m
    pairs = [(i, m) for i in range(n_dp) for m in range(n_mp)]
    first_hop = [(i * n_mp + m, side(i, m) if m % 2 == 0 else lower(i, m)) for i, m in pairs]
    second_hop = [(i * n_mp + m, lower(i, m) if m % 2 == 0 else side(i, m)) for i, m in pairs]
    high_groups = [[h * 4 + low for h in range(n_hi)] for low in range(4)]
    data_groups = [
        [h * 4 + low * 2 + y for h in range(n_hi) for y in range(2)] for low in range(2)
    ]

    def gather_tokens(own):
        near = lax.ppermute(own, BOTH, first_hop)
        two = jnp.concatenate([own, near], axis=0)
        four = jnp.concatenate([two, lax.ppermute(two, BOTH, second_hop)], axis=0)
        return jnp.concatenate([four, lax.ppermute(four, "mp", core_swap)], axis=0)

    def scatter_tokens(left, right, contract):
        half = left.shape[0] // 2
        part = half // 4
        arrived = lax.ppermute(
            dot(left[half:], right, contract).astype(bf16), "mp", core_swap
        )
        four = dot(left[:half], right, contract) + arrived.astype(f32)
        arrived = lax.ppermute(four[2 * part :].astype(bf16), BOTH, second_hop)
        two = four[: 2 * part] + arrived.astype(f32)
        arrived = lax.ppermute(two[part:].astype(bf16), BOTH, first_hop)
        return two[:part] + arrived.astype(f32)

    def on_device(
        tokens,
        text,
        image_seg,
        text_seg,
        w_qkv,
        w_out,
        c_q,
        c_kv,
        c_out,
        w_up,
        w_down,
        norm_gain,
        norm_bias,
        out_bias,
        up_bias,
        cotangent,
    ):
        d, m = lax.axis_index("dp"), lax.axis_index("mp")
        high, low, near_y = d // 4, (d // 2) % 2, d % 2
        core = m % 2
        seq, dim = tokens.shape
        text_len, text_dim = text_seg.shape[1], text.shape[1] * n_mp
        block = seq // 8
        place = low * 4 + m
        slice_dim = dim // n_dp
        slice_text = text_dim // n_dp
        mine = w_qkv.shape[2] // 2
        hidden = w_up.shape[1] // 2
        heads = mine // HD

        def xor_order(masks):
            return (d ^ jnp.array(masks, jnp.int32)).astype(jnp.int32)

        def ordered(own, theirs, axis=0):
            return jnp.where(
                low == 0, jnp.stack([own, theirs], axis), jnp.stack([theirs, own], axis)
            )

        def swap_low(values):
            return lax.ppermute(values, "dp", flip[2])

        def cut(parts, shape):
            def side_of(g):
                pieces = []
                for weight, kind in parts:
                    axis = 0 if kind == "col" else weight.ndim - 1
                    width = weight.shape[axis] // 2
                    pieces.append(lax.dynamic_slice_in_dim(weight, g * width, width, axis))
                return (jnp.stack(pieces) if len(pieces) > 1 else pieces[0]).reshape(shape)

            return side_of(low), side_of(1 - low)

        def spread(keep, recv):
            pair = jnp.stack([keep, recv])
            if n_hi == 2:
                far = lax.all_gather(pair, "dp", axis=0, axis_index_groups=high_groups)
                far = pick(far, 1 - high)
                return [
                    pair,
                    far,
                    lax.ppermute(pair, "dp", flip[1]),
                    lax.ppermute(far, "dp", flip[1]),
                ]
            pair = jnp.where(low == 0, pair, pair[::-1])
            own = lax.all_gather(pair, "dp", axis=0, axis_index_groups=high_groups)
            theirs = lax.ppermute(own, "dp", flip[1])
            full = jnp.where(
                near_y == 0, jnp.stack([own, theirs], 2), jnp.stack([theirs, own], 2)
            )
            return full.reshape((n_dp,) + keep.shape)

        def assemble(pieces, kinds, shapes):
            units = len(kinds)
            if n_hi != 2:
                outs = [[] for _ in shapes]
                for unit, (which, kind, _) in enumerate(kinds):
                    value = pieces[:, unit] if units > 1 else pieces
                    if kind == "col":
                        value = jnp.moveaxis(value, 0, 1)
                    outs[which].append(value.reshape(shapes[which][0], -1))
                return [jnp.concatenate(out, axis=1) for out in outs]

            return assembled(xor_order([0, 2, 4, 6, 1, 3, 5, 7]), pieces, kinds, shapes, n_dp)

        def all_blocks(terms):
            if n_hi != 2:
                return ()
            j = jnp.arange(8, dtype=jnp.int32)
            order = (j // 4 * 4 + (low ^ (j % 2)) * 2 + j // 2 % 2).astype(jnp.int32)
            return (grad_blocks(order, terms, n_dp, [8])[0],)

        def scattered(terms, blocks, axis):
            if n_hi != 2:
                return collected(terms, (), (), axis)
            total = lax.psum_scatter(
                blocks[0].reshape((4, 2) + blocks[0].shape[1:]),
                "dp",
                scatter_dimension=0,
                axis_index_groups=data_groups,
            )
            total = with_layout_constraint(total, Layout((0, 1, 2)))
            return ordered(total[0].astype(f32), swap_low(total[1]).astype(f32), axis)

        def first_blocks(terms):
            if n_hi != 2:
                return ()
            return (grad_blocks(xor_order([5, 7, 1, 3]), terms, n_dp, [4])[0],)

        def second_blocks(terms, away, *gates):
            if n_hi != 2:
                return ()
            arrived = after(lax.ppermute(away[0], "dp", flip[1]), *gates)
            return tuple(grad_blocks(xor_order([4, 6, 0, 2]), terms, n_dp, [2, 2], arrived))

        def across_high(second, *gates):
            if n_hi != 2:
                return ()
            return (after(lax.ppermute(second[0], "dp", flip[4]), *gates),)

        def collected(terms, second, arrived, axis):
            if n_hi == 2:
                total = second[1].astype(f32) + arrived[0].astype(f32)
                own, theirs = total[0], swap_low(total[1].astype(bf16))
            else:
                grads = []
                for kind, lefts, rights in terms:
                    cut_of = lambda v: v[0][v[1] * v[2] : v[1] * (v[2] + 1)]
                    grad = sum(
                        dot(cut_of(left), cut_of(right), ((0,), (0,)))
                        for left, right in zip(lefts, rights)
                    ).astype(bf16)
                    if kind == "row":
                        grads.append(grad.reshape(n_dp, -1, grad.shape[1]))
                    else:
                        grads.append(
                            jnp.moveaxis(grad.reshape(grad.shape[0], n_dp, -1), 1, 0)
                        )
                grad = jnp.concatenate(grads, axis=2)
                grad = grad.reshape((n_hi, 2, 2) + grad.shape[1:])
                arrived = lax.ppermute(pick(grad, 1 - near_y, 2), "dp", flip[1])
                total = (pick(grad, near_y, 2).astype(f32) + arrived.astype(f32)).astype(bf16)
                total = lax.psum_scatter(
                    total, "dp", scatter_dimension=0, axis_index_groups=high_groups
                )
                theirs = swap_low(pick(total, 1 - low))
                own = pick(total, low).astype(f32)
            return ordered(own, theirs.astype(f32), axis)

        qkv_shape = (3, slice_dim, mine)
        stay_qkv, go_qkv = cut([(w_qkv, "row")], qkv_shape)
        got_qkv = swap_low(go_qkv)
        packed = slice_dim == mine
        if packed:
            stay_proj, go_proj = cut(
                [(w_out, "col"), (c_q, "row"), (c_out, "col")], (3, slice_dim, mine)
            )
        else:
            singles = [
                cut([(w_out, "col")], (mine, slice_dim)),
                cut([(c_q, "row")], (slice_dim, mine)),
                cut([(c_out, "col")], (mine, slice_dim)),
            ]
        stay_kv, go_kv = cut([(c_kv, "row")], (2, slice_text, mine))
        stay_up, go_up = cut([(w_up, "row")], (slice_dim, hidden))
        stay_down, go_down = cut([(w_down, "col")], (hidden, slice_dim))
        pieces_qkv = spread(stay_qkv, got_qkv)
        far = lambda pieces, *which: tuple(pieces[i] for i in which) if n_hi == 2 else ()
        full_qkv = assemble(pieces_qkv, [(0, "row", j) for j in range(3)], [(dim, 3 * mine)])[0]
        kinds, shapes = ("col", "row", "col"), [(mine, dim), (dim, mine), (mine, dim)]
        if packed:
            got_proj = swap_low(after(go_proj, got_qkv))
            pieces_proj = spread(stay_proj, got_proj)
            full_out, full_cq, full_cout = assemble(
                pieces_proj, [(i, kind, 0) for i, kind in enumerate(kinds)], shapes
            )
        else:
            got_proj = got_qkv
            pieces_proj = [got_qkv] * 2
            full_out, full_cq, full_cout = [
                assemble(spread(stay, swap_low(go)), [(0, kind, 0)], [shape])[0]
                for (stay, go), kind, shape in zip(singles, kinds, shapes)
            ]
        got_kv = swap_low(after(go_kv, got_proj))
        pieces_kv = spread(stay_kv, got_kv)
        full_kv = assemble(pieces_kv, [(0, "row", 0), (0, "row", 1)], [(text_dim, 2 * mine)])[0]
        bias_up = lax.dynamic_slice(up_bias, (low * hidden,), (hidden,))

        local = after(jnp.stack([tokens, cotangent]), got_qkv)
        own = lax.dynamic_slice(local, (0, place * block, 0), (2, block, dim))
        away = lax.dynamic_slice(
            local, (0, ((1 - low) * 4 + m) * block, 0), (2, block, dim)
        )
        both = ordered(own, swap_low(away))
        segs = jnp.concatenate([image_seg[0], text_seg[0]])
        segs = ordered(segs, swap_low(segs))
        order = jnp.where(
            core == 0,
            jnp.array([0, 2, 4, 6, 1, 5, 3, 7], jnp.int32),
            jnp.array([0, 4, 2, 6, 1, 3, 5, 7], jnp.int32),
        )
        image_ids = jnp.take(segs[:, :seq].reshape(2, 8, block), place ^ order, axis=1)
        image_ids = image_ids.reshape(2, seq)
        text_ids = segs[:, seq:]
        words = lax.all_gather(ordered(text, swap_low(text)), "mp", axis=2, tiled=True)
        words = words.reshape(2 * text_len, text_dim)

        rows = (0, 1)
        residual = [both[r, 0].astype(f32) for r in rows]
        upstream = [both[r, 1].astype(f32) for r in rows]
        q_ids = [image_ids[r].reshape(seq, 1) for r in rows]
        i_ids = [image_ids[r].reshape(1, seq) for r in rows]
        t_ids = [text_ids[r].reshape(1, text_len) for r in rows]

        def norm(values, which):
            out, pull = jax.vjp(normalize, values, norm_gain[which], norm_bias[which])
            return out.astype(bf16), pull

        straight, across = ((1,), (0,)), ((1,), (1,))
        pulls = [[None] * 2 for _ in range(4)]
        hid_one, qkv, mixed, after_self = [], [], [], []
        for r in rows:
            normed, pulls[0][r] = norm(residual[r], 0)
            hid_one.append(gather_tokens(normed))
        hid_one[0] = after(hid_one[0], got_kv)
        got_up = swap_low(after(go_up, hid_one[1]))
        got_down = swap_low(after(go_down, hid_one[1]))
        pieces_up = spread(stay_up, got_up)
        full_up = assemble(pieces_up, [(0, "row", 0)], [(dim, hidden)])[0]
        pieces_down = spread(stay_down, got_down)
        full_down = assemble(pieces_down, [(0, "col", 0)], [(hidden, dim)])[0]
        for r in rows:
            qkv.append(dot(hid_one[r], full_qkv, straight).astype(bf16))
            mixed.append(attend(qkv[r], qkv[r], 0, heads, q_ids[r], i_ids[r], heads))
            ready = after(mixed[r], got_up, got_down, *far(pieces_kv, 1)) if r == 0 else mixed[r]
            after_self.append(
                residual[r] + scatter_tokens(ready, full_out, straight) + out_bias[0]
            )
        hid_two, cross_q, cross_mixed, after_cross = [], [], [], []
        cross_kv = dot(after(words, *far(pieces_up, 1, 2)), full_kv, straight).astype(bf16)
        for r in rows:
            normed, pulls[1][r] = norm(after_self[r], 1)
            hid_two.append(gather_tokens(after(normed, words) if r else normed))
        for r in rows:
            cross_q.append(dot(hid_two[r], full_cq, straight).astype(bf16))
            cross_mixed.append(attend(cross_q[r], cross_kv, r, 0, q_ids[r], t_ids[r], heads))
            after_cross.append(
                after_self[r] + scatter_tokens(cross_mixed[r], full_cout, straight) + out_bias[1]
            )
        hid_three, pre_act, act, after_mlp = [], [], [], []
        for r in rows:
            normed, pulls[2][r] = norm(after_cross[r], 2)
            gates = far(pieces_down, 2) if r else far(pieces_up, 3) + far(pieces_down, 1)
            hid_three.append(gather_tokens(after(normed, *gates)))
        for r in rows:
            pre_act.append(dot(hid_three[r], full_up, straight) + bias_up)
            act.append(gelu_tanh(pre_act[r]).astype(bf16))
            after_mlp.append(
                after_cross[r] + scatter_tokens(act[r], full_down, straight) + out_bias[2]
            )

        gains, shifts, biases = [0.0] * 4, [0.0] * 4, [0.0] * 3

        def back_norm(which, r, grad):
            out, gain, shift = pulls[which][r](grad)
            gains[which] = gains[which] + gain
            shifts[which] = shifts[which] + shift
            return out

        outs, grad_mlp, low_mlp = [], [], []
        for r in rows:
            final, pulls[3][r] = norm(after_mlp[r], 3)
            outs.append(final)
            grad_mlp.append(back_norm(3, r, upstream[r]))
            biases[2] = biases[2] + jnp.sum(grad_mlp[r], axis=0)
            low_mlp.append(gather_tokens(grad_mlp[r].astype(bf16)))
        def streams(values):
            return [(value, value.shape[0], 0) for value in values]

        down_term = [("col", streams(act), streams(low_mlp))]
        down = first_blocks(down_term)
        grad_pre, grad_in = [], []
        for r in rows:
            ready = low_mlp[r] if r == 0 else after(low_mlp[r], *down)
            grad_act = dot(ready, full_down, across)
            grad_pre.append(jax.vjp(gelu_tanh, pre_act[r])[1](grad_act)[0].astype(bf16))
            grad_in.append(scatter_tokens(grad_pre[r], full_up, across))
        up_term = [("row", streams(hid_three), streams(grad_pre))]
        up = first_blocks(up_term)
        grad_after_cross, low_cross = [], []
        for r in rows:
            grad_after_cross.append(grad_mlp[r] + back_norm(2, r, grad_in[r]))
            biases[1] = biases[1] + jnp.sum(grad_after_cross[r], axis=0)
            ready = grad_after_cross[r].astype(bf16)
            low_cross.append(gather_tokens(ready if r == 0 else after(ready, *up)))
        up_grad = jnp.sum(grad_pre[0].astype(f32), axis=0) + jnp.sum(
            grad_pre[1].astype(f32), axis=0
        )

        down_second = second_blocks(down_term, down, *grad_in)
        cq_low, ckv_low, grad_in = [], [], []
        for r in rows:
            ready = after(low_cross[r], *down_second) if r == 0 else low_cross[r]
            grad_mixed = dot(ready, full_cout, across).astype(bf16)
            dq, dkv = attend_back(
                cross_q[r], cross_kv, r, 0, grad_mixed, q_ids[r], t_ids[r], heads
            )
            cq_low.append(dq)
            ckv_low.append(dkv)
            grad_in.append(scatter_tokens(dq, full_cq, across))
        cq_term = ("row", streams(hid_two), streams(cq_low))
        cout_term = ("col", streams(cross_mixed), streams(low_cross))
        kv_term = [("row", [(words, text_len, r) for r in rows], streams(ckv_low))]
        both_term = [cq_term, cout_term]
        both_first, kv_first = first_blocks(both_term), first_blocks(kv_term)
        grad_after_self, low_self = [], []
        for r in rows:
            grad_after_self.append(grad_after_cross[r] + back_norm(1, r, grad_in[r]))
            biases[0] = biases[0] + jnp.sum(grad_after_self[r], axis=0)
            ready = grad_after_self[r].astype(bf16)
            if r == 1:
                up_second = second_blocks(up_term, up, *cq_low)
            gates = kv_first + up_second if r else both_first
            low_self.append(gather_tokens(after(ready, *gates)))
        text_term = dot(jnp.concatenate(ckv_low), full_kv, across).astype(bf16)

        down_far = across_high(down_second, *cq_low)
        out_term = [("col", streams(mixed), streams(low_self))]
        out_first = first_blocks(out_term)
        both_second = second_blocks(both_term, both_first, *grad_after_self)
        qkv_low = []
        for r in rows:
            gates = (*down_far, text_term, *out_first) if r else both_second
            grad_mixed = dot(after(low_self[r], *gates), full_out, across).astype(bf16)
            qkv_low.append(
                attend_back(qkv[r], qkv[r], 0, heads, grad_mixed, q_ids[r], i_ids[r], heads)[0]
            )
        qkv_term = [("row", streams(hid_one), streams(qkv_low))]
        qkv_first = all_blocks(qkv_term)
        up_far = across_high(up_second, *qkv_first)
        kv_second = second_blocks(kv_term, kv_first, *qkv_first)
        out_second = second_blocks(out_term, out_first, *kv_second)
        both_far = across_high(both_second, *kv_second)
        kv_far = across_high(kv_second, *out_second)
        out_far = across_high(out_second)
        grad_tokens = []
        for r in rows:
            grad_in = scatter_tokens(after(qkv_low[r], *qkv_first), full_qkv, across)
            piece = grad_after_self[r] + back_norm(0, r, grad_in)
            grad_tokens.append(piece)
        text_term = lax.psum_scatter(
            text_term.reshape(2, text_len, text_dim), "mp", scatter_dimension=2, tiled=True
        )
        grad_text = pick(text_term, low).astype(f32) + swap_low(
            pick(text_term, 1 - low)
        ).astype(f32)

        sum_down = collected(down_term, down_second, down_far, 0)
        sum_up = collected(up_term, up_second, up_far, 1)
        if packed:
            sum_both = collected(both_term, both_second, both_far, 0)
            sum_cq = jnp.moveaxis(sum_both[:, :, :mine], 0, 1)
            sum_cout = sum_both[:, :, mine:]
        else:
            sum_cq, sum_cout = collected([cq_term], (), (), 1), collected([cout_term], (), (), 0)
        sum_kv = collected(kv_term, kv_second, kv_far, 1)
        sum_out = collected(out_term, out_second, out_far, 0)
        sum_qkv = scattered(qkv_term, qkv_first, 1)

        small = jnp.stack(gains + shifts + biases)
        small = small + lax.ppermute(small, "mp", core_swap)
        small = small + lax.ppermute(small, "mp", side_swap)
        wide = jnp.concatenate([small.reshape(-1), up_grad])
        if n_hi == 2:
            for bit in (1, 4):
                wide = wide + lax.ppermute(wide, "dp", flip[bit])
        else:
            wide = wide + lax.ppermute(wide, "dp", flip[1])
            wide = lax.psum(wide, "dp", axis_index_groups=high_groups)
        theirs = swap_low(wide)
        parts = (wide + theirs)[: 11 * dim].reshape(11, dim)
        up_total = ordered(wide[11 * dim :], theirs[11 * dim :]).reshape(-1)

        def whole_row(pieces):
            pieces = jnp.stack(pieces)
            pieces = ordered(pick(pieces, low), swap_low(pick(pieces, 1 - low)))
            pieces = lax.all_gather(pieces, "mp", axis=1)
            return pieces.reshape(seq, dim)

        output = whole_row(outs)
        grad_tokens = [piece.astype(bf16) for piece in grad_tokens]
        grad_tokens = whole_row([piece for piece in grad_tokens]).astype(f32)
        gain_total, shift_total, bias_total = parts[:4], parts[4:8], parts[8:]

        apart = lambda v, n: v.reshape(v.shape[0], 2, n, -1).transpose(2, 0, 1, 3)
        return (
            output,
            grad_tokens,
            grad_text,
            apart(sum_qkv, 3).reshape(w_qkv.shape),
            sum_out.reshape(w_out.shape),
            sum_cq.reshape(c_q.shape),
            apart(sum_kv, 2).reshape(c_kv.shape),
            sum_cout.reshape(c_out.shape),
            sum_up.reshape(w_up.shape),
            sum_down.reshape(w_down.shape),
            gain_total,
            shift_total,
            bias_total,
            up_total,
        )

    return on_device


def solution(mesh):
    in_specs = (
        P("dp", None),
        P("dp", "mp"),
        P("dp", None),
        P("dp", None),
        P(None, "dp", "mp"),
        P("mp", "dp"),
        P("dp", "mp"),
        P(None, "dp", "mp"),
        P("mp", "dp"),
        P("dp", "mp"),
        P("mp", "dp"),
        P(),
        P(),
        P(),
        P("mp"),
        P("dp", None),
    )
    out_specs = (
        P("dp", None),
        P("dp", None),
        P("dp", "mp"),
        P(None, "dp", "mp"),
        P("mp", "dp"),
        P("dp", "mp"),
        P(None, "dp", "mp"),
        P("mp", "dp"),
        P("dp", "mp"),
        P("mp", "dp"),
        P(),
        P(),
        P(),
        P("mp"),
    )
    return jax.shard_map(
        build(mesh.shape["dp"], mesh.shape["mp"]),
        mesh=mesh,
        in_specs=in_specs,
        out_specs=out_specs,
        check_vma=False,
    )
```
